128 devices in a mesh: chain: 32 (over x, z, core), arc: 4 (over y).
Axes of the slice: x: 4, y: 4, z: 4, core: 2. Of those that a mesh axis runs over, the one named last changes fastest.
Arguments:
- design: bfloat16 [262144, 512], P(('chain', 'arc')), may hold values from -0.125 to 0.125
- observed: bfloat16 [262144, 512], P(('chain', 'arc')), may hold values from -6 to 6
- row_interval: int32 [262144], P(('chain', 'arc')), may hold values from 0 to 3
- prior_ridge: float32 [128, 512], P(('chain', 'arc')), may hold values from 0.1 to 1
- coupling: float32 [128, 512], P(('chain', 'arc')), may hold values from 1 to 8
Outputs:
- solution: float32 [128, 512, 512], P(('chain', 'arc'))
- residual: float32 [262144, 512], P(('chain', 'arc'))
The draws below stay inside these ranges and needn't reach their ends.
Inputs may be any that keep to these rules, and one draw needn't show every extreme that they name: `row_interval`: every row's interval lies in the arc of the device that holds the row.
All inputs are finite; a program needn't handle non-finite values.
Results may differ from the reference program's by a relative error of at most 0.00046.
Values may be sent and summed in bfloat16 or wider, within the bound.
No kernel may reach another device: no remote copies, remote signals or barrier semaphores. Data moves between devices by JAX's collectives and lax.ppermute only.
A program may use at most 128 MiB of HBM per device.

```python
import math
import jax
import jax.numpy as jnp
from jax import lax

STATES = 512
REPLICAS = 512
ROWS_DEV = 2048
ARC_LEN = 4
INTERVALS = 128
ROWS = 262144


def plant(entries, own_key, least, largest):
    longest = entries.shape.index(max(entries.shape))
    spots = []
    for shift in (0, 1):
        where = [jax.random.randint(jax.random.fold_in(own_key, axis), (), 0, length) for axis, length in enumerate(entries.shape)]
        where[longest] = (where[longest] + shift) % entries.shape[longest]
        spots.append(tuple(where))
    return entries.at[spots[0]].set(least).at[spots[1]].set(largest)


def block_levels(rng, shape, shards, least, largest):
    def one(dim, shards_of):
        steps = jax.random.uniform(jax.random.fold_in(jax.random.fold_in(rng, 6), dim), (shards_of,), jnp.float32, least / len(shards), largest / len(shards))
        return jnp.repeat(jnp.exp(steps), shape[dim] // shards_of).reshape((-1,) + (1,) * (len(shape) - dim - 1))

    gain = one(*shards[0])
    for cut in shards[1:]:
        gain = gain * one(*cut)
    return gain


def scatter_about(key, extent, deviation, most, split=(), kind=jnp.bfloat16):
    array = jax.random.normal(key, extent, jnp.float32) * deviation
    if len(split) > 0:
        array = block_levels(key, extent, split, -0.22, 0.18) * array
    return jnp.clip(array, min=-most, max=most).astype(kind)


def setup_inputs(seed: int = 0) -> dict:
    key_of = jax.random.split(jax.random.key(seed), 6)
    return {
        "design": scatter_about(key_of[0], (ROWS, STATES), ROWS_DEV ** -0.5, 0.125, ((0, 128),)),
        "observed": scatter_about(key_of[1], (ROWS, REPLICAS), 1.0, 6.0, ((0, 128),)),
        "row_interval": plant(jax.random.randint(key_of[2], (ROWS,), 0, ARC_LEN), jax.random.fold_in(key_of[2], 1), 0, ARC_LEN - 1).astype(jnp.int32),
        "prior_ridge": jnp.clip(jnp.exp(math.log(1.0) - 2.3025851 * jax.random.uniform(key_of[3], (INTERVALS, STATES), jnp.float32) ** block_levels(key_of[3], (INTERVALS, STATES), ((0, 128),), -0.2, 0.2)), 0.1, 1.0),
        "coupling": jnp.clip(jnp.exp(math.log(8.0) - 2.0794415 * jax.random.uniform(key_of[4], (INTERVALS, STATES), jnp.float32) ** block_levels(key_of[4], (INTERVALS, STATES), ((0, 128),), -0.2, 0.2)), 1.0, 8.0),
    }


def cholesky_apply(matrix, columns):
    factor = jnp.linalg.cholesky(matrix)
    middle = jax.scipy.linalg.solve_triangular(factor, columns, lower=True)
    return jax.scipy.linalg.solve_triangular(factor, middle, lower=True, trans=1)

def shifted(stacked, distance):
    filler = jnp.zeros((abs(distance),) + stacked.shape[1:], stacked.dtype)
    if distance > 0:
        return jnp.concatenate([filler, stacked[:-distance]], axis=0)
    return jnp.concatenate([stacked[-distance:], filler], axis=0)

def reference(design, observed, row_interval, prior_ridge, coupling):
    arc_count = INTERVALS // ARC_LEN
    arc_rows = ROWS_DEV * ARC_LEN
    highest = lax.Precision.HIGHEST
    slot_ids = jnp.arange(ARC_LEN, dtype=jnp.int32)
    design_arcs = design.reshape(arc_count, arc_rows, STATES)
    joined = jnp.concatenate([design, observed], axis=1).reshape(arc_count, arc_rows, STATES + REPLICAS)
    row_picks = row_interval.reshape(arc_count, arc_rows)[:, :, None] == slot_ids[None, None, :]

    def widen(design_arc, picks_arc):
        return jnp.where(picks_arc[:, :, None], design_arc[:, None, :], jnp.zeros((), jnp.bfloat16)).reshape(arc_rows, ARC_LEN * STATES)

    def arc_normals(operands):
        design_arc, joined_arc, picks_arc = operands
        wide_rows = widen(design_arc, picks_arc)
        return lax.dot_general(wide_rows.astype(jnp.float32), joined_arc.astype(jnp.float32), (((0,), (0,)), ((), ())), preferred_element_type=jnp.float32)
    normals = lax.map(arc_normals, (design_arcs, joined, row_picks)).reshape(INTERVALS, STATES, STATES + REPLICAS)
    gram_block = normals[:, :, :STATES]
    right_side = normals[:, :, STATES:]
    right_link = jnp.concatenate([coupling[:-1], jnp.zeros((1, STATES), jnp.float32)], axis=0)
    left_link = shifted(right_link, 1)
    identity = jnp.eye(STATES, dtype=jnp.float32)
    blocks = gram_block + identity[None, :, :] * (prior_ridge + left_link + right_link)[:, None, :]

    def first_solve(operands):
        matrix, side = operands
        return cholesky_apply(matrix, jnp.concatenate([identity, side], axis=1))
    first = lax.map(first_solve, (blocks, right_side))
    inverse = first[:, :, :STATES]
    local_solve = first[:, :, STATES:]
    inverse_prev = shifted(inverse, 1)
    inverse_next = shifted(inverse, -1)
    solve_prev = shifted(local_solve, 1)
    solve_next = shifted(local_solve, -1)
    left_prev = shifted(left_link, 1)
    right_next = shifted(right_link, -1)
    lower_block = -(left_link[:, :, None] * inverse_prev * left_prev[:, None, :])
    upper_block = -(right_link[:, :, None] * inverse_next * right_next[:, None, :])
    block_one = blocks - left_link[:, :, None] * inverse_prev * left_link[:, None, :] - right_link[:, :, None] * inverse_next * right_link[:, None, :]
    side_one = right_side + left_link[:, :, None] * solve_prev + right_link[:, :, None] * solve_next

    def second_solve(operands):
        matrix, lower_one, upper_one, side = operands
        return cholesky_apply(matrix, jnp.concatenate([lower_one, upper_one, side], axis=1))
    second = lax.map(second_solve, (block_one, lower_block, upper_block, side_one))
    upper_solves = second[:, :, STATES:]
    lower_solves = jnp.concatenate([second[:, :, :STATES], second[:, :, 2 * STATES:]], axis=2)
    far_below = shifted(upper_solves, 2)
    far_above = shifted(lower_solves, -2)
    from_lower = jnp.matmul(lower_block, far_below, precision=highest)
    from_upper = jnp.matmul(upper_block, far_above, precision=highest)
    block_two = block_one - from_lower[:, :, :STATES] - from_upper[:, :, :STATES]
    side_two = side_one - from_lower[:, :, STATES:] - from_upper[:, :, STATES:]

    def final_solve(operands):
        matrix, side = operands
        return cholesky_apply(matrix, side)
    solution = lax.map(final_solve, (block_two, side_two))
    rounded = solution.astype(jnp.bfloat16).reshape(arc_count, ARC_LEN * STATES, REPLICAS)

    def arc_predict(operands):
        design_arc, picks_arc, rounded_arc = operands
        return jnp.dot(widen(design_arc, picks_arc).astype(jnp.float32), rounded_arc.astype(jnp.float32), preferred_element_type=jnp.float32)
    predicted = lax.map(arc_predict, (design_arcs, row_picks, rounded)).reshape(ROWS, REPLICAS)
    residual = observed.astype(jnp.float32) - predicted
    return (solution, residual)
```

```python
import functools

import jax
import jax.numpy as jnp
from jax import lax
from jax.experimental import pallas as pl
from jax.experimental.pallas import tpu as pltpu
from jax.sharding import PartitionSpec as P

F32 = jnp.float32
BF16 = jnp.bfloat16
PAIR = ("chain", "arc")


def from_behind(value, axis, steps):
    count = lax.axis_size(axis)
    first, last = (max(0, -steps), min(count, count - steps))
    return lax.ppermute(value, axis, [(source, source + steps) for source in range(first, last)])


def around(value, steps):
    count = lax.axis_size("arc")
    return lax.ppermute(value, "arc", [(source, (source + steps) % count) for source in range(count)])


def dot1(a, b):
    return lax.dot_general(a, b, (((1,), (0,)), ((), ())), preferred_element_type=F32)


def split(x):
    high = x.astype(BF16)
    return high, (x - high.astype(F32)).astype(BF16)


def dot3(a, b):
    (ah, al), (bh, bl) = a, b
    return dot1(ah, bh) + (dot1(ah, bl) + dot1(al, bh))


def dot_full(a, b):
    return lax.dot_general(
        a, b, (((1,), (0,)), ((), ())), precision=lax.Precision.HIGHEST, preferred_element_type=F32
    )


def eye_mask(n):
    return lax.broadcasted_iota(jnp.int32, (n, n), 0) == lax.broadcasted_iota(jnp.int32, (n, n), 1)


def to_column(row, eye):
    return jnp.sum(jnp.where(eye, row, 0.0), axis=1, keepdims=True)


def invert(b_ref, x_ref, r_ref, bh_ref, bl_ref):
    n = b_ref.shape[0]
    eye = eye_mask(n)
    one = jnp.where(eye, 1.0, 0.0).astype(F32)
    b = b_ref[...]
    picked = jnp.where(eye, b, 0.0)
    s_row = lax.rsqrt(jnp.sum(picked, axis=0, keepdims=True))
    s_col = lax.rsqrt(jnp.sum(picked, axis=1, keepdims=True))
    b = b * s_row * s_col
    b_ref[...] = b
    high, low = split(b)
    bh_ref[...] = high
    bl_ref[...] = low
    r0 = one - b
    r0_low = r0.astype(BF16)
    square = dot1(r0_low, r0_low)
    bound = jnp.max(jnp.sum(jnp.abs(square), axis=1, keepdims=True))
    well = bound < 0.6

    @pl.when(well)
    def _():
        x_ref[...] = (one + r0) + dot1((one + r0).astype(BF16), square.astype(BF16))

        def step(carry):
            count, _ = carry
            residual = jnp.where(eye_mask(n), 1.0, 0.0) - dot3(
                (bh_ref[...], bl_ref[...]), split(x_ref[...])
            )
            r_ref[...] = residual.astype(BF16)
            x_ref[...] += dot1(x_ref[...].astype(BF16), r_ref[...])
            return count + 1, jnp.sum(residual * residual)

        lax.while_loop(
            lambda carry: jnp.logical_and(carry[0] < 12, carry[1] > 1.6e-5),
            step,
            (jnp.int32(0), jnp.float32(1.0)),
        )

    @pl.when(jnp.logical_not(well))
    def _():
        largest = jnp.max(jnp.sum(jnp.abs(b_ref[...]), axis=1, keepdims=True))
        alpha = 2.0 / (1.0 + largest)
        x_ref[...] = jnp.where(eye_mask(n), alpha, 0.0)

        def step(carry):
            count, _ = carry
            residual = jnp.where(eye_mask(n), 1.0, 0.0) - dot_full(b_ref[...], x_ref[...])
            x_ref[...] += dot_full(x_ref[...], residual)
            return count + 1, jnp.sum(residual * residual)

        lax.while_loop(
            lambda carry: jnp.logical_and(carry[0] < 60, carry[1] > 1e-7),
            step,
            (jnp.int32(0), jnp.float32(1.0)),
        )

    x_ref[...] = x_ref[...] * s_row * s_col


def scratch_of(n):
    return [
        pltpu.VMEM((n, n), F32),
        pltpu.VMEM((n, n), F32),
        pltpu.VMEM((n, n), BF16),
        pltpu.VMEM((n, n), BF16),
        pltpu.VMEM((n, n), BF16),
    ]


def first_kernel(own, one, two, three, vec, b_out, f_out, g_out, s_out, b_ref, x_ref, r_ref, bh, bl):
    n = own.shape[0]
    eye = eye_mask(n)
    diagonal = vec[0:1, :] + vec[1:2, :] + vec[2:3, :]
    total = (own[...] + one[...]) + (two[...] + three[...])
    block = total[:, :n] + jnp.where(eye, diagonal, 0.0)
    b_out[...] = block
    b_ref[...] = block
    f_out[...] = total[:, n:]
    invert(b_ref, x_ref, r_ref, bh, bl)
    g_out[...] = x_ref[...]
    s_out[0:n, :] = dot3(split(x_ref[...]), split(f_out[...]))
    s_out[n : n + 8, :] = vec[...]


def second_kernel(b, f, g_low, s_low, g_high, s_high, vec, b_out, f_out, h_out, t_out, b_ref, x_ref, r_ref, bh, bl):
    n = b.shape[0]
    eye = eye_mask(n)
    left, right = vec[1:2, :], vec[2:3, :]
    left_col, right_col = to_column(left, eye), to_column(right, eye)
    block = b[...] - (left_col * g_low[...]) * left - (right_col * g_high[...]) * right
    b_out[...] = block
    b_ref[...] = block
    f_out[...] = f[...] + left_col * s_low[0:n, :] + right_col * s_high[0:n, :]
    invert(b_ref, x_ref, r_ref, bh, bl)
    h_out[...] = x_ref[...]
    t_out[...] = dot3(split(x_ref[...]), split(f_out[...]))


def third_kernel(b, f, g_low, v_low, g_high, v_high, h_low, t_low, h_high, t_high, vec, out, out16, b_ref, x_ref, r_ref, bh, bl):
    n = b.shape[0]
    eye = eye_mask(n)
    b_ref[...] = b[...]
    x_ref[...] = f[...]
    for g, near, far, h, t in (
        (g_low, vec[1:2, :], v_low[1:2, :], h_low, t_low),
        (g_high, vec[2:3, :], v_high[2:3, :], h_high, t_high),
    ):
        near_col, far_col = to_column(near, eye), to_column(far, eye)
        link = split((near_col * g[...]) * far)
        link_t = split((far_col * g[...]) * near)
        half = dot3(link, split(h[...]))
        b_ref[...] -= dot3(split(half), link_t)
        x_ref[...] += dot3(link, split(t[...]))
    out[...] = x_ref[...]
    invert(b_ref, x_ref, r_ref, bh, bl)
    value = dot3(split(x_ref[...]), split(out[...]))
    out[...] = value
    out16[...] = value.astype(BF16)


def call(kernel, outs, n, *args):
    return pl.pallas_call(
        kernel,
        out_shape=outs,
        scratch_shapes=scratch_of(n),
    )(*args)


def per_device(design, observed, row_interval, prior_ridge, coupling):
    row_count, n = design.shape
    slot_count = lax.axis_size("arc")
    is_last = lax.axis_index(PAIR) == lax.axis_size(PAIR) - 1
    right_link = jnp.where(is_last, jnp.zeros_like(coupling), coupling)
    left_link = from_behind(coupling, PAIR, 1)
    vec = jnp.concatenate([prior_ridge, left_link, right_link, jnp.zeros((5, n), F32)], axis=0)
    place = lax.axis_index("arc")
    joined = jnp.concatenate([design, observed], axis=1)
    parts = []
    for shift in (2, 1, 3, 0):
        pick = row_interval == (place + shift) % slot_count
        picked = jnp.where(pick[:, None], design, jnp.zeros((), design.dtype))
        part = lax.dot_general(picked, joined, (((0,), (0,)), ((), ())), preferred_element_type=F32)
        parts.append(around(part, shift) if shift else part)
    square = jax.ShapeDtypeStruct((n, n), F32)
    tall = jax.ShapeDtypeStruct((n + 8, n), F32)
    block, side, inverse, solve = call(
        first_kernel, (square, square, square, tall), n, parts[3], parts[0], parts[1], parts[2], vec
    )
    g_low, g_high = from_behind(inverse, PAIR, 1), from_behind(inverse, PAIR, -1)
    s_low, s_high = from_behind(solve, PAIR, 1), from_behind(solve, PAIR, -1)
    block_one, side_one, inverse_one, solve_one = call(
        second_kernel, (square, square, square, square), n, block, side, g_low, s_low, g_high, s_high, vec
    )
    h_low, h_high = from_behind(inverse_one, PAIR, 2), from_behind(inverse_one, PAIR, -2)
    t_low, t_high = from_behind(solve_one, PAIR, 2), from_behind(solve_one, PAIR, -2)
    solution, rounded = call(
        third_kernel,
        (square, jax.ShapeDtypeStruct((n, n), BF16)),
        n,
        block_one,
        side_one,
        g_low,
        s_low[n:],
        g_high,
        s_high[n:],
        h_low,
        t_low,
        h_high,
        t_high,
        vec,
    )
    residual = observed.astype(F32)
    for shift in (0, 1, 3, 2):
        state = around(rounded, -shift % slot_count) if shift else rounded
        pick = row_interval == (place + shift) % slot_count
        picked = jnp.where(pick[:, None], design, jnp.zeros((), design.dtype))
        residual = residual - jnp.dot(picked, state, preferred_element_type=F32)
    return (solution[None], residual)


def solution(mesh):
    placed = (P(PAIR, None), P(PAIR, None), P(PAIR), P(PAIR, None), P(PAIR, None))
    return jax.shard_map(
        per_device,
        mesh=mesh,
        in_specs=placed,
        out_specs=(P(PAIR, None, None), P(PAIR, None)),
        check_vma=False,
    )
```

```python
import functools

import jax
import jax.numpy as jnp
from jax import lax
from jax.experimental import pallas as pl
from jax.experimental.pallas import tpu as pltpu
from jax.sharding import PartitionSpec as P

F32 = jnp.float32
BF16 = jnp.bfloat16
PAIR = ("chain", "arc")


def from_behind(value, axis, steps):
    count = lax.axis_size(axis)
    first, last = (max(0, -steps), min(count, count - steps))
    return lax.ppermute(value, axis, [(source, source + steps) for source in range(first, last)])


def around(value, steps):
    count = lax.axis_size("arc")
    return lax.ppermute(value, "arc", [(source, (source + steps) % count) for source in range(count)])


def dot1(a, b):
    return lax.dot_general(a, b, (((1,), (0,)), ((), ())), preferred_element_type=F32)


def split(x):
    high = x.astype(BF16)
    return high, (x - high.astype(F32)).astype(BF16)


def dot3(a, b):
    (ah, al), (bh, bl) = a, b
    return dot1(ah, bh) + (dot1(ah, bl) + dot1(al, bh))


def dot_full(a, b):
    return lax.dot_general(
        a, b, (((1,), (0,)), ((), ())), precision=lax.Precision.HIGHEST, preferred_element_type=F32
    )


def eye_mask(n):
    return lax.broadcasted_iota(jnp.int32, (n, n), 0) == lax.broadcasted_iota(jnp.int32, (n, n), 1)


def to_column(row, eye):
    return jnp.sum(jnp.where(eye, row, 0.0), axis=1, keepdims=True)


def invert(b_ref, x_ref, r_ref, bh_ref, bl_ref):
    n = b_ref.shape[0]
    eye = eye_mask(n)
    one = jnp.where(eye, 1.0, 0.0).astype(F32)
    b = b_ref[...]
    picked = jnp.where(eye, b, 0.0)
    s_row = lax.rsqrt(jnp.sum(picked, axis=0, keepdims=True))
    s_col = lax.rsqrt(jnp.sum(picked, axis=1, keepdims=True))
    b = b * s_row * s_col
    b_ref[...] = b
    high, low = split(b)
    bh_ref[...] = high
    bl_ref[...] = low
    x_ref[...] = one - b
    r0 = x_ref[...].astype(BF16)
    square = dot1(r0, r0)
    well = jnp.sum(square * square) < 0.9
    r_ref[...] = square.astype(BF16)

    @pl.when(well)
    def _():
        x_ref[...] += jnp.where(eye_mask(n), 1.0, 0.0)
        x_ref[...] += dot1(x_ref[...].astype(BF16), r_ref[...])
        fourth = dot1(r_ref[...], r_ref[...]).astype(BF16)
        x_ref[...] += dot1(x_ref[...].astype(BF16), fourth)

        def step(carry):
            count, _ = carry
            residual = jnp.where(eye_mask(n), 1.0, 0.0) - dot3(
                (bh_ref[...], bl_ref[...]), split(x_ref[...])
            )
            r_ref[...] = residual.astype(BF16)
            x_ref[...] += dot1(x_ref[...].astype(BF16), r_ref[...])
            return count + 1, jnp.sum(residual * residual)

        lax.while_loop(
            lambda carry: jnp.logical_and(carry[0] < 12, carry[1] > 4e-5),
            step,
            (jnp.int32(0), jnp.float32(1.0)),
        )

    @pl.when(jnp.logical_not(well))
    def _():
        largest = jnp.max(jnp.sum(jnp.abs(b_ref[...]), axis=1, keepdims=True))
        alpha = 2.0 / (1.0 + largest)
        x_ref[...] = jnp.where(eye_mask(n), alpha, 0.0)

        def step(carry):
            count, _ = carry
            residual = jnp.where(eye_mask(n), 1.0, 0.0) - dot_full(b_ref[...], x_ref[...])
            x_ref[...] += dot_full(x_ref[...], residual)
            return count + 1, jnp.sum(residual * residual)

        lax.while_loop(
            lambda carry: jnp.logical_and(carry[0] < 60, carry[1] > 1e-7),
            step,
            (jnp.int32(0), jnp.float32(1.0)),
        )

    x_ref[...] = x_ref[...] * s_row * s_col


STEP = 128
GRAIN = 1.0 / 128.0
FULL = 32767.0
MSG = (256, 1792)
EDGES = ((0, 512, 640, 1152, 1664), (0, 384, 640, 1152, 1664))


def encode(msg, rows, pieces):
    lane = lax.broadcasted_iota(jnp.int32, (STEP, STEP), 1)
    scales = jnp.zeros((STEP, STEP), jnp.int32)
    for number, (piece, start) in enumerate(zip(pieces, EDGES[rows])):
        top = jnp.maximum(jnp.max(jnp.abs(piece), axis=1, keepdims=True), 1e-30)
        power = jnp.ceil(jnp.log2(top) * STEP)
        unit = jnp.exp2(power * (-GRAIN)) * FULL
        value = jnp.clip(jnp.round(piece * unit), -FULL, FULL).astype(jnp.int32)
        msg[rows * STEP : rows * STEP + STEP, start : start + piece.shape[1]] = value.astype(jnp.int16)
        scales = jnp.where(lane == number, power.astype(jnp.int32), scales)
    msg[rows * STEP : rows * STEP + STEP, 1664:1792] = scales.astype(jnp.int16)


def encode_all(msg, matrix, side):
    encode(msg, 0, (matrix[384:512, :], matrix[0:128, 0:128], side[0:128, :], side[256:384, :]))
    encode(msg, 1, (matrix[256:384, 0:384], matrix[128:256, 0:256], side[128:256, :], side[384:512, :]))


def decode(msg, rows):
    scales = msg[rows * STEP : rows * STEP + STEP, 1664:1792].astype(jnp.int32).astype(F32)
    scales = jnp.exp2(scales * GRAIN) * (1.0 / FULL)
    edges = EDGES[rows]
    for number in range(4):
        value = msg[rows * STEP : rows * STEP + STEP, edges[number] : edges[number + 1]]
        yield value.astype(jnp.int32).astype(F32) * scales[:, number : number + 1]


SPOTS = (
    ((384, 512), (0, 128), (0, 512), (256, 512)),
    ((256, 384), (128, 256), (128, 512), (384, 512)),
)


def unpack(msgs, matrix, side, add):
    for rows in range(2):
        for number, pieces in enumerate(zip(*(decode(msg, rows) for msg in msgs))):
            start, width = SPOTS[rows][number]
            target = matrix if number < 2 else side
            value = functools.reduce(lambda p, q: p + q, pieces)
            if add:
                value = value + target[start : start + STEP, 0:width]
            target[start : start + STEP, 0:width] = value
    for i in range(4):
        for j in range(i):
            matrix[j * STEP : j * STEP + STEP, i * STEP : i * STEP + STEP] = matrix[
                i * STEP : i * STEP + STEP, j * STEP : j * STEP + STEP
            ].T


def scratch_of(n):
    return [
        pltpu.VMEM((n, n), F32),
        pltpu.VMEM((n, n), F32),
        pltpu.VMEM((n, n), BF16),
        pltpu.VMEM((n, n), BF16),
        pltpu.VMEM((n, n), BF16),
    ]


def masked(slot, row_interval, turned):
    pick = jnp.where(row_interval[...] == slot[0], 1.0, 0.0).astype(BF16)
    return turned[...] * pick


def gram_send(slot, row_interval, turned, design, observed, msg):
    left = masked(slot, row_interval, turned)
    d, o = design[...], observed[...]
    for rows in range(2):
        pieces = []
        for number, (start, width) in enumerate(SPOTS[rows]):
            other = d[:, 0:width] if number < 2 else o
            pieces.append(dot1(left[start : start + STEP, :], other))
        encode(msg, rows, pieces)


def gram_first(slot, row_interval, design, observed, turned, msg):
    turned[...] = design[...].T
    gram_send(slot, row_interval, turned, design, observed, msg)


def gram_own(slot, row_interval, turned, design, observed, matrix, side):
    left = masked(slot, row_interval, turned)
    matrix[...] = dot1(left, design[...])
    side[...] = dot1(left, observed[...])


def first_kernel(own_n, own_f, one, two, three, vec, b_out, f_out, msg, b_ref, x_ref, r_ref, bh, bl):
    n = own_n.shape[0]
    diagonal = vec[0:1, :] + vec[1:2, :] + vec[2:3, :]
    b_ref[...] = own_n[...]
    f_out[...] = own_f[...]
    unpack((one, two, three), b_ref, f_out, True)
    b_ref[...] += jnp.where(eye_mask(n), diagonal, 0.0)
    b_out[...] = b_ref[...]
    invert(b_ref, x_ref, r_ref, bh, bl)
    b_ref[...] = dot3(split(x_ref[...]), split(f_out[...]))
    encode_all(msg, x_ref, b_ref)


def second_kernel(b, f, low, high, vec, b_out, f_out, up, down, b_ref, x_ref, r_ref, bh, bl):
    n = b.shape[0]
    eye = eye_mask(n)
    left, right = vec[1:2, :], vec[2:3, :]
    left_col, right_col = to_column(left, eye), to_column(right, eye)
    unpack((low,), b_ref, x_ref, False)
    b_out[...] = b[...] - (left_col * b_ref[...]) * left
    f_out[...] = f[...] + left_col * x_ref[...]
    unpack((high,), b_ref, x_ref, False)
    b_out[...] -= (right_col * b_ref[...]) * right
    f_out[...] += right_col * x_ref[...]
    b_ref[...] = b_out[...]
    invert(b_ref, x_ref, r_ref, bh, bl)
    b_ref[...] = dot3(split(x_ref[...]), split(f_out[...]))
    encode_all(up, (right_col * x_ref[...]) * right, right_col * b_ref[...])
    encode_all(down, (left_col * x_ref[...]) * left, left_col * b_ref[...])


def third_kernel(b, f, low, high, far_low, far_high, vec, out, out16, g_ref, h_ref, t_ref, b_ref, x_ref, r_ref, bh, bl):
    n = b.shape[0]
    eye = eye_mask(n)
    b_ref[...] = b[...]
    out[...] = f[...]
    for near, far, link in ((low, far_low, vec[1:2, :]), (high, far_high, vec[2:3, :])):
        link_col = to_column(link, eye)
        unpack((near,), g_ref, x_ref, False)
        unpack((far,), h_ref, t_ref, False)
        g = split(g_ref[...])
        half = dot3(g, split(h_ref[...]))
        b_ref[...] -= (link_col * dot3(split(half), g)) * link
        out[...] += link_col * dot3(g, split(t_ref[...]))
    invert(b_ref, x_ref, r_ref, bh, bl)
    value = dot3(split(x_ref[...]), split(out[...]))
    out[...] = value
    out16[...] = value.astype(BF16)


def call(kernel, outs, n, *args, extra=()):
    return pl.pallas_call(kernel, out_shape=outs, scratch_shapes=list(extra) + scratch_of(n))(*args)


def gram(kernel, outs, slot, *args):
    specs = [pl.BlockSpec(memory_space=pltpu.SMEM)] + [pl.BlockSpec(memory_space=pltpu.VMEM)] * len(args)
    return pl.pallas_call(kernel, out_shape=outs, in_specs=specs)(slot, *args)


def per_device(design, observed, row_interval, prior_ridge, coupling):
    row_count, n = design.shape
    slot_count = lax.axis_size("arc")
    is_last = lax.axis_index(PAIR) == lax.axis_size(PAIR) - 1
    right_link = jnp.where(is_last, jnp.zeros_like(coupling), coupling)
    left_link = from_behind(coupling, PAIR, 1)
    vec = jnp.concatenate([prior_ridge, left_link, right_link, jnp.zeros((5, n), F32)], axis=0)
    place = lax.axis_index("arc")
    square = jax.ShapeDtypeStruct((n, n), F32)
    message = jax.ShapeDtypeStruct(MSG, jnp.int16)
    flat = row_interval.reshape(1, row_count)

    def slot(shift):
        return ((place + shift) % slot_count).astype(jnp.int32).reshape(1)

    turned, part = gram(
        gram_first, (jax.ShapeDtypeStruct((n, row_count), BF16), message), slot(2), flat, design, observed
    )
    parts = [around(part, 2)]
    for shift in (1, 3):
        part = gram(gram_send, message, slot(shift), flat, turned, design, observed)
        parts.append(around(part, shift))
    own = gram(gram_own, (square, square), slot(0), flat, turned, design, observed)
    block, side, near = call(first_kernel, (square, square, message), n, *own, *parts, vec)
    low, high = from_behind(near, PAIR, 1), from_behind(near, PAIR, -1)
    block_one, side_one, up, down = call(
        second_kernel, (square, square, message, message), n, block, side, low, high, vec
    )
    far_low, far_high = from_behind(up, PAIR, 2), from_behind(down, PAIR, -2)
    solution, rounded = call(
        third_kernel,
        (square, jax.ShapeDtypeStruct((n, n), BF16)),
        n,
        block_one,
        side_one,
        low,
        high,
        far_low,
        far_high,
        vec,
        extra=[pltpu.VMEM((n, n), F32)] * 3,
    )
    residual = observed.astype(F32)
    for shift in (0, 1, 3, 2):
        state = around(rounded, -shift % slot_count) if shift else rounded
        pick = row_interval == (place + shift) % slot_count
        picked = jnp.where(pick[:, None], design, jnp.zeros((), design.dtype))
        residual = residual - jnp.dot(picked, state, preferred_element_type=F32)
    return (solution[None], residual)


def solution(mesh):
    placed = (P(PAIR, None), P(PAIR, None), P(PAIR), P(PAIR, None), P(PAIR, None))
    return jax.shard_map(
        per_device,
        mesh=mesh,
        in_specs=placed,
        out_specs=(P(PAIR, None, None), P(PAIR, None)),
        check_vma=False,
    )
```

```python
import functools

import jax
import jax.numpy as jnp
from jax import lax
from jax.experimental import pallas as pl
from jax.experimental.pallas import tpu as pltpu
from jax.sharding import PartitionSpec as P

F32 = jnp.float32
BF16 = jnp.bfloat16
PAIR = ("chain", "arc")


SLOTS = 4
LINE = 2 * SLOTS


def seat(t):
    line, spot = t // LINE, t % LINE
    return (2 * line + spot % 2) * SLOTS + spot // 2


def carry(value, source_of, target_of):
    count = lax.axis_size(PAIR)
    pairs = [(source_of(t), target_of(t)) for t in range(count)]
    return lax.ppermute(value, PAIR, [pair for pair in pairs if pair[1] is not None])


def along(value, steps):
    count = lax.axis_size(PAIR)
    return carry(value, seat, lambda t: seat(t + steps) if 0 <= t + steps < count else None)


def home(t):
    return t


def to_seat(value, m):
    return carry(value, lambda t: t - t % SLOTS + (t % SLOTS ^ m), seat)


def to_arc(value, m):
    return carry(value, seat, lambda t: t - t % SLOTS + (t % SLOTS ^ m))


def dot1(a, b):
    return lax.dot_general(a, b, (((1,), (0,)), ((), ())), preferred_element_type=F32)


def split(x):
    high = x.astype(BF16)
    return high, (x - high.astype(F32)).astype(BF16)


def dot3(a, b):
    (ah, al), (bh, bl) = a, b
    return dot1(ah, bh) + (dot1(ah, bl) + dot1(al, bh))


def dot_full(a, b):
    return lax.dot_general(
        a, b, (((1,), (0,)), ((), ())), precision=lax.Precision.HIGHEST, preferred_element_type=F32
    )


def eye_mask(n):
    return lax.broadcasted_iota(jnp.int32, (n, n), 0) == lax.broadcasted_iota(jnp.int32, (n, n), 1)


def to_column(row, eye):
    return jnp.sum(jnp.where(eye, row, 0.0), axis=1, keepdims=True)


def invert(b_ref, x_ref, r_ref, q_ref, bh_ref, bl_ref):
    n = b_ref.shape[0]
    eye = eye_mask(n)
    one = jnp.where(eye, 1.0, 0.0).astype(F32)
    b = b_ref[...]
    picked = jnp.where(eye, b, 0.0)
    s_row = lax.rsqrt(jnp.sum(picked, axis=0, keepdims=True))
    s_col = lax.rsqrt(jnp.sum(picked, axis=1, keepdims=True))
    b = b * s_row * s_col
    b_ref[...] = b
    high, low = split(b)
    bh_ref[...] = high
    bl_ref[...] = low
    x_ref[...] = one - b
    r0 = x_ref[...].astype(BF16)
    square = dot1(r0, r0)
    r_ref[...] = square.astype(BF16)
    fourth = dot1(r_ref[...], r_ref[...])
    well = jnp.sum(fourth * fourth) < 0.9
    q_ref[...] = fourth.astype(BF16)

    @pl.when(well)
    def _():
        x_ref[...] += jnp.where(eye_mask(n), 1.0, 0.0)
        x_ref[...] += dot1(x_ref[...].astype(BF16), r_ref[...])
        x_ref[...] += dot1(x_ref[...].astype(BF16), q_ref[...])

        def step(carry):
            count, _ = carry
            residual = jnp.where(eye_mask(n), 1.0, 0.0) - dot3(
                (bh_ref[...], bl_ref[...]), split(x_ref[...])
            )
            r_ref[...] = residual.astype(BF16)
            x_ref[...] += dot1(x_ref[...].astype(BF16), r_ref[...])
            return count + 1, jnp.sum(residual * residual)

        lax.while_loop(
            lambda carry: jnp.logical_and(carry[0] < 12, carry[1] > 4e-5),
            step,
            (jnp.int32(0), jnp.float32(1.0)),
        )

    @pl.when(jnp.logical_not(well))
    def _():
        largest = jnp.max(jnp.sum(jnp.abs(b_ref[...]), axis=1, keepdims=True))
        alpha = 2.0 / (1.0 + largest)
        x_ref[...] = jnp.where(eye_mask(n), alpha, 0.0)

        def step(carry):
            count, _ = carry
            residual = jnp.where(eye_mask(n), 1.0, 0.0) - dot_full(b_ref[...], x_ref[...])
            x_ref[...] += dot_full(x_ref[...], residual)
            return count + 1, jnp.sum(residual * residual)

        lax.while_loop(
            lambda carry: jnp.logical_and(carry[0] < 60, carry[1] > 1e-7),
            step,
            (jnp.int32(0), jnp.float32(1.0)),
        )

    x_ref[...] = x_ref[...] * s_row * s_col


STEP = 128
GRAIN = 1.0 / 128.0
FULL = 32767.0
FINE = 4194304.0
SHIFT = 13000.0
MSG = (210, 16, 128)
EDGES = ((0, 4, 5, 9, 13), (0, 3, 5, 9, 13))
BLOCKS = 13


def power_of(size):
    return jnp.ceil(jnp.log2(jnp.maximum(size, 1e-30)) * STEP)


def to_tiles(value):
    return jnp.clip(jnp.round(value), -FULL, FULL).astype(jnp.int32).astype(jnp.int16)


def encode(msg, rows, pieces):
    lane = lax.broadcasted_iota(jnp.int32, (STEP, STEP), 1)
    eye = eye_mask(STEP)
    scales = jnp.zeros((STEP, STEP), F32)
    for number, piece in enumerate(pieces):
        blocks = [piece[:, i : i + STEP] for i in range(0, piece.shape[1], STEP)]
        if number < 2:
            own = jnp.sum(jnp.where(eye, blocks[-1], 0.0), axis=1, keepdims=True)
            blocks[-1] = jnp.where(eye, 0.0, blocks[-1])
            power = power_of(jnp.abs(own))
            fine = (own * jnp.exp2(power * (-GRAIN)) - 1.0) * FINE
            scales = jnp.where(lane == 4 + number, power + SHIFT, scales)
            scales = jnp.where(lane == 6 + number, fine, scales)
        size = functools.reduce(jnp.maximum, [jnp.abs(block) for block in blocks])
        power = power_of(jnp.max(size, axis=1, keepdims=True))
        unit = jnp.exp2(power * (-GRAIN)) * FULL
        scales = jnp.where(lane == number, power + SHIFT, scales)
        for i, block in enumerate(blocks):
            place = 8 * (BLOCKS * rows + EDGES[rows][number] + i)
            msg[place : place + 8] = to_tiles(block * unit).reshape(8, 16, STEP)
    msg[208 + rows] = to_tiles(scales.T[0:16, :])


def encode_all(msg, matrix, side):
    encode(msg, 0, (matrix[384:512, :], matrix[0:128, 0:128], side[0:128, :], side[256:384, :]))
    encode(msg, 1, (matrix[256:384, 0:384], matrix[128:256, 0:256], side[128:256, :], side[384:512, :]))


def decode(msg, rows):
    eye = eye_mask(STEP)
    flat = msg[208 + rows].astype(jnp.int32).astype(F32)
    codes = jnp.concatenate([flat, jnp.zeros((STEP - 16, STEP), F32)], axis=0).T
    powers = jnp.exp2((codes - SHIFT) * GRAIN)
    for number in range(4):
        unit = powers[:, number : number + 1] * (1.0 / FULL)
        blocks = []
        for i in range(EDGES[rows][number], EDGES[rows][number + 1]):
            place = 8 * (BLOCKS * rows + i)
            blocks.append(msg[place : place + 8].reshape(STEP, STEP).astype(jnp.int32).astype(F32) * unit)
        if number < 2:
            own = powers[:, 4 + number : 5 + number] * (1.0 + codes[:, 6 + number : 7 + number] * (1.0 / FINE))
            blocks[-1] = jnp.where(eye, own, blocks[-1])
        yield jnp.concatenate(blocks, axis=1)


SPOTS = (
    ((384, 512), (0, 128), (0, 512), (256, 512)),
    ((256, 384), (128, 256), (128, 512), (384, 512)),
)


def unpack(msgs, matrix, side):
    for rows in range(2):
        for number, pieces in enumerate(zip(*(decode(msg, rows) for msg in msgs))):
            start, width = SPOTS[rows][number]
            target = matrix if number < 2 else side
            value = functools.reduce(lambda p, q: p + q, pieces)
            target[start : start + STEP, 0:width] = value
    for i in range(4):
        for j in range(i):
            matrix[j * STEP : j * STEP + STEP, i * STEP : i * STEP + STEP] = matrix[
                i * STEP : i * STEP + STEP, j * STEP : j * STEP + STEP
            ].T


def scratch_of(n):
    return [
        pltpu.VMEM((n, n), F32),
        pltpu.VMEM((n, n), F32),
        pltpu.VMEM((n, n), BF16),
        pltpu.VMEM((n, n), BF16),
        pltpu.VMEM((n, n), BF16),
        pltpu.VMEM((n, n), BF16),
    ]


def masked(slot, row_interval, turned):
    pick = jnp.where(row_interval[...] == slot[0], 1.0, 0.0).astype(BF16)
    return turned[...] * pick


def gram_send(slot, row_interval, turned, design, observed, msg):
    left = masked(slot, row_interval, turned)
    d, o = design[...], observed[...]
    for rows in range(2):
        pieces = []
        for number, (start, width) in enumerate(SPOTS[rows]):
            other = d[:, 0:width] if number < 2 else o
            pieces.append(dot1(left[start : start + STEP, :], other))
        encode(msg, rows, pieces)


def gram_first(slot, row_interval, design, observed, turned, msg):
    turned[...] = design[...].T
    gram_send(slot, row_interval, turned, design, observed, msg)


def first_kernel(one, two, three, four, vec, b_out, f_out, msg, b_ref, x_ref, r_ref, q_ref, bh, bl):
    n = b_out.shape[0]
    diagonal = vec[0:1, :] + vec[1:2, :] + vec[2:3, :]
    unpack((one, two, three, four), b_ref, f_out)
    b_ref[...] += jnp.where(eye_mask(n), diagonal, 0.0)
    b_out[...] = b_ref[...]
    invert(b_ref, x_ref, r_ref, q_ref, bh, bl)
    b_ref[...] = dot3(split(x_ref[...]), split(f_out[...]))
    encode_all(msg, x_ref, b_ref)


def second_kernel(b, f, low, high, vec, b_out, f_out, up, down, b_ref, x_ref, r_ref, q_ref, bh, bl):
    n = b.shape[0]
    eye = eye_mask(n)
    left, right = vec[1:2, :], vec[2:3, :]
    left_col, right_col = to_column(left, eye), to_column(right, eye)
    unpack((low,), b_ref, x_ref)
    b_out[...] = b[...] - (left_col * b_ref[...]) * left
    f_out[...] = f[...] + left_col * x_ref[...]
    unpack((high,), b_ref, x_ref)
    b_out[...] -= (right_col * b_ref[...]) * right
    f_out[...] += right_col * x_ref[...]
    b_ref[...] = b_out[...]
    invert(b_ref, x_ref, r_ref, q_ref, bh, bl)
    b_ref[...] = dot3(split(x_ref[...]), split(f_out[...]))
    encode_all(up, (right_col * x_ref[...]) * right, right_col * b_ref[...])
    encode_all(down, (left_col * x_ref[...]) * left, left_col * b_ref[...])


def third_kernel(b, f, low, high, far_low, far_high, vec, out, out16, g_ref, h_ref, t_ref, b_ref, x_ref, r_ref, q_ref, bh, bl):
    n = b.shape[0]
    eye = eye_mask(n)
    b_ref[...] = b[...]
    out[...] = f[...]
    for near, far, link in ((low, far_low, vec[1:2, :]), (high, far_high, vec[2:3, :])):
        link_col = to_column(link, eye)
        unpack((near,), g_ref, x_ref)
        unpack((far,), h_ref, t_ref)
        g = split(g_ref[...])
        half = dot3(g, split(h_ref[...]))
        b_ref[...] -= (link_col * dot3(split(half), g)) * link
        out[...] += link_col * dot3(g, split(t_ref[...]))
    invert(b_ref, x_ref, r_ref, q_ref, bh, bl)
    value = dot3(split(x_ref[...]), split(out[...]))
    out[...] = value
    out16[...] = value.astype(BF16)


def call(kernel, outs, n, *args, extra=()):
    return pl.pallas_call(kernel, out_shape=outs, scratch_shapes=list(extra) + scratch_of(n))(*args)


def gram(kernel, outs, slot, *args):
    specs = [pl.BlockSpec(memory_space=pltpu.SMEM)] + [pl.BlockSpec(memory_space=pltpu.VMEM)] * len(args)
    return pl.pallas_call(kernel, out_shape=outs, in_specs=specs)(slot, *args)


def per_device(design, observed, row_interval, prior_ridge, coupling):
    row_count, n = design.shape
    count = lax.axis_size(PAIR)
    chain, place = lax.axis_index("chain"), lax.axis_index("arc")
    time = LINE * (chain // 2) + 2 * place + chain % 2
    mine = carry(jnp.concatenate([prior_ridge, coupling], axis=0), home, seat)
    left_link = carry(coupling, home, lambda t: seat(t + 1) if t + 1 < count else None)
    right_link = jnp.where(time == count - 1, 0.0, mine[1:2])
    vec = jnp.concatenate([mine[0:1], left_link, right_link, jnp.zeros((5, n), F32)], axis=0)
    square = jax.ShapeDtypeStruct((n, n), F32)
    message = jax.ShapeDtypeStruct(MSG, jnp.int16)
    flat = row_interval.reshape(1, row_count)

    def slot(m):
        return (place ^ m).astype(jnp.int32).reshape(1)

    turned, part = gram(
        gram_first, (jax.ShapeDtypeStruct((n, row_count), BF16), message), slot(2), flat, design, observed
    )
    parts = [to_seat(part, 2)]
    for m in (3, 1, 0):
        part = gram(gram_send, message, slot(m), flat, turned, design, observed)
        parts.append(to_seat(part, m))
    block, side, near = call(first_kernel, (square, square, message), n, *parts, vec)
    low, high = along(near, 1), along(near, -1)
    block_one, side_one, up, down = call(
        second_kernel, (square, square, message, message), n, block, side, low, high, vec
    )
    far_low, far_high = along(up, 2), along(down, -2)
    state, rounded = call(
        third_kernel,
        (square, jax.ShapeDtypeStruct((n, n), BF16)),
        n,
        block_one,
        side_one,
        low,
        high,
        far_low,
        far_high,
        vec,
        extra=[pltpu.VMEM((n, n), F32)] * 3,
    )
    solution = to_arc(state, 0)
    residual = observed.astype(F32)
    for m in range(SLOTS):
        state = to_arc(rounded, m) if m else solution.astype(BF16)
        picked = jnp.where((row_interval == (place ^ m))[:, None], design, jnp.zeros((), design.dtype))
        residual = residual - jnp.dot(picked, state, preferred_element_type=F32)
    return (solution[None], residual)


def solution(mesh):
    placed = (P(PAIR, None), P(PAIR, None), P(PAIR), P(PAIR, None), P(PAIR, None))
    return jax.shard_map(
        per_device,
        mesh=mesh,
        in_specs=placed,
        out_specs=(P(PAIR, None, None), P(PAIR, None)),
        check_vma=False,
    )
```

```python
import functools

import jax
import jax.numpy as jnp
from jax import lax
from jax.experimental import pallas as pl
from jax.experimental.pallas import tpu as pltpu
from jax.sharding import PartitionSpec as P

F32 = jnp.float32
BF16 = jnp.bfloat16
PAIR = ("chain", "arc")


SLOTS = 4
LINE = 2 * SLOTS


def seat(t):
    line, spot = t // LINE, t % LINE
    return (2 * line + spot % 2) * SLOTS + spot // 2


def carry(value, source_of, target_of):
    count = lax.axis_size(PAIR)
    pairs = [(source_of(t), target_of(t)) for t in range(count)]
    return lax.ppermute(value, PAIR, [pair for pair in pairs if pair[1] is not None])


def along(value, steps):
    count = lax.axis_size(PAIR)
    return carry(value, seat, lambda t: seat(t + steps) if 0 <= t + steps < count else None)


def home(t):
    return t


def to_seat(value, m):
    return carry(value, lambda t: t - t % SLOTS + (t % SLOTS ^ m), seat)


def to_arc(value, m):
    return carry(value, seat, lambda t: t - t % SLOTS + (t % SLOTS ^ m))


def dot1(a, b):
    return lax.dot_general(a, b, (((1,), (0,)), ((), ())), preferred_element_type=F32)


def split(x):
    high = x.astype(BF16)
    return high, (x - high.astype(F32)).astype(BF16)


def dot3(a, b):
    (ah, al), (bh, bl) = a, b
    return dot1(ah, bh) + (dot1(ah, bl) + dot1(al, bh))


def dot_full(a, b):
    return lax.dot_general(
        a, b, (((1,), (0,)), ((), ())), precision=lax.Precision.HIGHEST, preferred_element_type=F32
    )


def eye_mask(n):
    return lax.broadcasted_iota(jnp.int32, (n, n), 0) == lax.broadcasted_iota(jnp.int32, (n, n), 1)


def to_column(row, eye):
    return jnp.sum(jnp.where(eye, row, 0.0), axis=1, keepdims=True)


def invert(b_ref, x_ref, r_ref, q_ref, bh_ref, bl_ref):
    n = b_ref.shape[0]
    eye = eye_mask(n)
    one = jnp.where(eye, 1.0, 0.0).astype(F32)
    b = b_ref[...]
    picked = jnp.where(eye, b, 0.0)
    s_row = lax.rsqrt(jnp.sum(picked, axis=0, keepdims=True))
    s_col = lax.rsqrt(jnp.sum(picked, axis=1, keepdims=True))
    b = b * s_row * s_col
    b_ref[...] = b
    high, low = split(b)
    bh_ref[...] = high
    bl_ref[...] = low
    x_ref[...] = one - b
    r0 = x_ref[...].astype(BF16)
    square = dot1(r0, r0)
    r_ref[...] = square.astype(BF16)
    fourth = dot1(r_ref[...], r_ref[...])
    well = jnp.sum(fourth * fourth) < 0.9
    q_ref[...] = fourth.astype(BF16)

    @pl.when(well)
    def _():
        x_ref[...] += jnp.where(eye_mask(n), 1.0, 0.0)
        x_ref[...] += dot1(x_ref[...].astype(BF16), r_ref[...])
        x_ref[...] += dot1(x_ref[...].astype(BF16), q_ref[...])

        def step(carry):
            count, _ = carry
            residual = jnp.where(eye_mask(n), 1.0, 0.0) - dot3(
                (bh_ref[...], bl_ref[...]), split(x_ref[...])
            )
            r_ref[...] = residual.astype(BF16)
            x_ref[...] += dot1(x_ref[...].astype(BF16), r_ref[...])
            return count + 1, jnp.sum(residual * residual)

        lax.while_loop(
            lambda carry: jnp.logical_and(carry[0] < 12, carry[1] > 4e-5),
            step,
            (jnp.int32(0), jnp.float32(1.0)),
        )

    @pl.when(jnp.logical_not(well))
    def _():
        largest = jnp.max(jnp.sum(jnp.abs(b_ref[...]), axis=1, keepdims=True))
        alpha = 2.0 / (1.0 + largest)
        x_ref[...] = jnp.where(eye_mask(n), alpha, 0.0)

        def step(carry):
            count, _ = carry
            residual = jnp.where(eye_mask(n), 1.0, 0.0) - dot_full(b_ref[...], x_ref[...])
            x_ref[...] += dot_full(x_ref[...], residual)
            return count + 1, jnp.sum(residual * residual)

        lax.while_loop(
            lambda carry: jnp.logical_and(carry[0] < 60, carry[1] > 1e-7),
            step,
            (jnp.int32(0), jnp.float32(1.0)),
        )

    x_ref[...] = x_ref[...] * s_row * s_col


STEP = 128
GRAIN = 1.0 / 128.0
FULL = 32767.0
FINE = 4194304.0
SHIFT = 13000.0
MATRIX = ((0, 80, ((384, 4), (0, 1))), (5, 81, ((256, 3), (128, 2))))
SIDE = ((0, 128, ((0, 4), (128, 4), (256, 4), (384, 4))),)
MATRIX_MSG = (82, 16, 128)
SIDE_MSG = (129, 16, 128)


def power_of(size):
    return jnp.ceil(jnp.log2(jnp.maximum(size, 1e-30)) * STEP)


def to_tiles(value):
    return jnp.clip(jnp.round(value), -FULL, FULL).astype(jnp.int32).astype(jnp.int16)


def encode(msg, plan, piece_of):
    lane = lax.broadcasted_iota(jnp.int32, (STEP, STEP), 1)
    eye = eye_mask(STEP)
    for first, spot, pieces in plan:
        scales = jnp.zeros((STEP, STEP), F32)
        place = 8 * first
        for number, (row, wide) in enumerate(pieces):
            piece = piece_of(row, wide * STEP)
            blocks = [piece[:, i * STEP : i * STEP + STEP] for i in range(wide)]
            if plan is MATRIX:
                own = jnp.sum(jnp.where(eye, blocks[-1], 0.0), axis=1, keepdims=True)
                blocks[-1] = jnp.where(eye, 0.0, blocks[-1])
                power = power_of(jnp.abs(own))
                fine = (own * jnp.exp2(power * (-GRAIN)) - 1.0) * FINE
                scales = jnp.where(lane == 4 + number, power + SHIFT, scales)
                scales = jnp.where(lane == 6 + number, fine, scales)
            size = functools.reduce(jnp.maximum, [jnp.abs(block) for block in blocks])
            power = power_of(jnp.max(size, axis=1, keepdims=True))
            unit = jnp.exp2(power * (-GRAIN)) * FULL
            scales = jnp.where(lane == number, power + SHIFT, scales)
            for block in blocks:
                msg[place : place + 8] = to_tiles(block * unit).reshape(8, 16, STEP)
                place += 8
        msg[spot] = to_tiles(scales.T[0:16, :])


def encode_ref(msg, plan, ref):
    encode(msg, plan, lambda row, width: ref[row : row + STEP, 0:width])


def decode(msg, plan):
    eye = eye_mask(STEP)
    for first, spot, pieces in plan:
        flat = msg[spot].astype(jnp.int32).astype(F32)
        codes = jnp.concatenate([flat, jnp.zeros((STEP - 16, STEP), F32)], axis=0).T
        powers = jnp.exp2((codes - SHIFT) * GRAIN)
        place = 8 * first
        for number, (row, wide) in enumerate(pieces):
            unit = powers[:, number : number + 1] * (1.0 / FULL)
            blocks = []
            for _ in range(wide):
                blocks.append(msg[place : place + 8].reshape(STEP, STEP).astype(jnp.int32).astype(F32) * unit)
                place += 8
            if plan is MATRIX:
                own = powers[:, 4 + number : 5 + number] * (1.0 + codes[:, 6 + number : 7 + number] * (1.0 / FINE))
                blocks[-1] = jnp.where(eye, own, blocks[-1])
            yield row, wide * STEP, jnp.concatenate(blocks, axis=1)


def unpack(msgs, plan, target):
    for pieces in zip(*(decode(msg, plan) for msg in msgs)):
        row, width, _ = pieces[0]
        target[row : row + STEP, 0:width] = functools.reduce(lambda p, q: p + q, [piece[2] for piece in pieces])
    if plan is MATRIX:
        for i in range(4):
            for j in range(i):
                target[j * STEP : j * STEP + STEP, i * STEP : i * STEP + STEP] = target[
                    i * STEP : i * STEP + STEP, j * STEP : j * STEP + STEP
                ].T


def scratch_of(n):
    return [
        pltpu.VMEM((n, n), F32),
        pltpu.VMEM((n, n), BF16),
        pltpu.VMEM((n, n), BF16),
        pltpu.VMEM((n, n), BF16),
        pltpu.VMEM((n, n), BF16),
    ]


def masked(slot, row_interval, turned):
    pick = jnp.where(row_interval[...] == slot, 1.0, 0.0).astype(BF16)
    return turned[...] * pick


ROUNDS = (2, 3, 1, 0)


def gram_matrix(place, row_interval, design, turned, *msgs):
    turned[...] = design[...].T
    for m, msg in zip(ROUNDS, msgs):
        left = masked(place[0] ^ m, row_interval, turned)
        encode(msg, MATRIX, lambda row, width: dot1(left[row : row + STEP, :], design[:, 0:width]))


def gram_side(rounds, place, row_interval, turned, observed, *msgs):
    for m, msg in zip(rounds, msgs):
        left = masked(place[0] ^ m, row_interval, turned)
        encode(msg, SIDE, lambda row, width: dot1(left[row : row + STEP, :], observed[...]))


def first_matrix(one, two, three, four, vec, b_out, x_out, msg, b_ref, r_ref, q_ref, bh, bl):
    n = b_out.shape[0]
    unpack((one, two, three, four), MATRIX, b_ref)
    b_ref[...] += jnp.where(eye_mask(n), vec[0:1, :] + vec[1:2, :] + vec[2:3, :], 0.0)
    b_out[...] = b_ref[...]
    invert(b_ref, x_out, r_ref, q_ref, bh, bl)
    encode_ref(msg, MATRIX, x_out)


def first_side(x, one, two, three, four, f_out, msg, t_ref):
    unpack((one, two, three, four), SIDE, f_out)
    t_ref[...] = dot3(split(x[...]), split(f_out[...]))
    encode_ref(msg, SIDE, t_ref)


def second_matrix(b, low, high, vec, b_out, x_out, up, down, b_ref, r_ref, q_ref, bh, bl):
    n = b.shape[0]
    eye = eye_mask(n)
    left, right = vec[1:2, :], vec[2:3, :]
    left_col, right_col = to_column(left, eye), to_column(right, eye)
    unpack((low,), MATRIX, b_ref)
    b_out[...] = b[...] - (left_col * b_ref[...]) * left
    unpack((high,), MATRIX, b_ref)
    b_out[...] -= (right_col * b_ref[...]) * right
    b_ref[...] = b_out[...]
    invert(b_ref, x_out, r_ref, q_ref, bh, bl)
    b_ref[...] = (right_col * x_out[...]) * right
    encode_ref(up, MATRIX, b_ref)
    b_ref[...] = (left_col * x_out[...]) * left
    encode_ref(down, MATRIX, b_ref)


def second_side(x, f, low, high, vec, f_out, up, down, t_ref):
    eye = eye_mask(f.shape[0])
    left_col, right_col = to_column(vec[1:2, :], eye), to_column(vec[2:3, :], eye)
    unpack((low,), SIDE, t_ref)
    f_out[...] = f[...] + left_col * t_ref[...]
    unpack((high,), SIDE, t_ref)
    f_out[...] += right_col * t_ref[...]
    value = dot3(split(x[...]), split(f_out[...]))
    t_ref[...] = right_col * value
    encode_ref(up, SIDE, t_ref)
    t_ref[...] = left_col * value
    encode_ref(down, SIDE, t_ref)


def third_matrix(b, low, high, far_low, far_high, vec, x_out, g_ref, h_ref, b_ref, r_ref, q_ref, bh, bl):
    n = b.shape[0]
    eye = eye_mask(n)
    b_ref[...] = b[...]
    for near, far, link in ((low, far_low, vec[1:2, :]), (high, far_high, vec[2:3, :])):
        unpack((near,), MATRIX, g_ref)
        unpack((far,), MATRIX, h_ref)
        g = split(g_ref[...])
        half = dot3(g, split(h_ref[...]))
        b_ref[...] -= (to_column(link, eye) * dot3(split(half), g)) * link
    invert(b_ref, x_out, r_ref, q_ref, bh, bl)


def third_side(x, f, low, high, far_low, far_high, vec, msg, out16, g_ref, t_ref, s_ref):
    eye = eye_mask(f.shape[0])
    s_ref[...] = f[...]
    for near, far, link in ((low, far_low, vec[1:2, :]), (high, far_high, vec[2:3, :])):
        unpack((near,), MATRIX, g_ref)
        unpack((far,), SIDE, t_ref)
        s_ref[...] += to_column(link, eye) * dot3(split(g_ref[...]), split(t_ref[...]))
    t_ref[...] = dot3(split(x[...]), split(s_ref[...]))
    encode_ref(msg, SIDE, t_ref)
    out16[...] = t_ref[...].astype(BF16)


def arrive(msg, out, out16):
    unpack((msg,), SIDE, out)
    out16[...] = out[...].astype(BF16)


def call(kernel, outs, scratch, *args):
    return pl.pallas_call(kernel, out_shape=outs, scratch_shapes=scratch)(*args)


def gram(kernel, outs, place, *args):
    specs = [pl.BlockSpec(memory_space=pltpu.SMEM)] + [pl.BlockSpec(memory_space=pltpu.VMEM)] * len(args)
    return pl.pallas_call(kernel, out_shape=outs, in_specs=specs)(place, *args)


def step_of(design, observed, row_interval, prior_ridge, coupling):
    row_count, n = design.shape
    count = lax.axis_size(PAIR)
    chain, place = lax.axis_index("chain"), lax.axis_index("arc")
    time = LINE * (chain // 2) + 2 * place + chain % 2
    square = jax.ShapeDtypeStruct((n, n), F32)
    half = jax.ShapeDtypeStruct((n, n), BF16)
    matrix_msg = jax.ShapeDtypeStruct(MATRIX_MSG, jnp.int16)
    side_msg = jax.ShapeDtypeStruct(SIDE_MSG, jnp.int16)
    flat = row_interval.reshape(1, row_count)
    where = place.astype(jnp.int32).reshape(1)
    plain = [pltpu.VMEM((n, n), F32)]
    work = scratch_of(n)

    turned, *parts = gram(
        gram_matrix, (jax.ShapeDtypeStruct((n, row_count), BF16),) + (matrix_msg,) * 4, where, flat, design
    )
    for i, m in enumerate(ROUNDS):
        parts[i] = to_seat(parts[i], m)
    side_parts = []
    for i in (0, 2):
        rounds = ROUNDS[i : i + 2]
        msgs = gram(functools.partial(gram_side, rounds), (side_msg,) * 2, where, flat, turned, observed)
        for j, m in enumerate(rounds):
            side_parts.append(to_seat(msgs[j], m))
    mine = carry(jnp.concatenate([prior_ridge, coupling], axis=0), home, seat)
    left_link = carry(coupling, home, lambda t: seat(t + 1) if t + 1 < count else None)
    right_link = jnp.where(time == count - 1, 0.0, mine[1:2])
    vec = jnp.concatenate([mine[0:1], left_link, right_link, jnp.zeros((5, n), F32)], axis=0)
    block, inverse, near = call(first_matrix, (square, square, matrix_msg), work, *parts, vec)
    low, high = along(near, 1), along(near, -1)
    side, near_side = call(first_side, (square, side_msg), plain, inverse, *side_parts)
    low_side, high_side = along(near_side, 1), along(near_side, -1)
    block_one, inverse_one, up, down = call(
        second_matrix, (square, square, matrix_msg, matrix_msg), work, block, low, high, vec
    )
    far_low, far_high = along(up, 2), along(down, -2)
    side_one, up_side, down_side = call(
        second_side, (square, side_msg, side_msg), plain, inverse_one, side, low_side, high_side, vec
    )
    far_low_side, far_high_side = along(up_side, 2), along(down_side, -2)
    inverse_two = call(third_matrix, square, plain * 2 + work, block_one, low, high, far_low, far_high, vec)
    code, rounded = call(
        third_side, (side_msg, half), plain * 3, inverse_two, side_one, low, high, far_low_side, far_high_side, vec
    )
    states = []
    for m in range(SLOTS):
        states.append(to_arc(rounded if m else code, m))
    solution, states[0] = call(arrive, (square, half), [], states[0])
    residual = observed.astype(F32)
    for m in range(SLOTS):
        picked = jnp.where((row_interval == (place ^ m))[:, None], design, jnp.zeros((), design.dtype))
        residual = residual - jnp.dot(picked, states[m], preferred_element_type=F32)
    return (solution[None], residual)


def solution(mesh):
    placed = (P(PAIR, None), P(PAIR, None), P(PAIR), P(PAIR, None), P(PAIR, None))
    return jax.shard_map(
        step_of,
        mesh=mesh,
        in_specs=placed,
        out_specs=(P(PAIR, None, None), P(PAIR, None)),
        check_vma=False,
    )
```

```python
import functools

import jax
import jax.numpy as jnp
from jax import lax
from jax.experimental import pallas as pl
from jax.experimental.pallas import tpu as pltpu
from jax.sharding import PartitionSpec as P

F32 = jnp.float32
BF16 = jnp.bfloat16
PAIR = ("chain", "arc")


SLOTS = 4
LINE = 2 * SLOTS


def seat(t):
    line, spot = t // LINE, t % LINE
    return (2 * line + spot % 2) * SLOTS + spot // 2


def carry(value, source_of, target_of):
    count = lax.axis_size(PAIR)
    pairs = [(source_of(t), target_of(t)) for t in range(count)]
    return lax.ppermute(value, PAIR, [pair for pair in pairs if pair[1] is not None])


def along(value, steps):
    count = lax.axis_size(PAIR)
    return carry(value, seat, lambda t: seat(t + steps) if 0 <= t + steps < count else None)


def home(t):
    return t


def to_seat(value, m):
    return carry(value, lambda t: t - t % SLOTS + (t % SLOTS ^ m), seat)


def to_arc(value, m):
    return carry(value, seat, lambda t: t - t % SLOTS + (t % SLOTS ^ m))


def dot1(a, b):
    return lax.dot_general(a, b, (((1,), (0,)), ((), ())), preferred_element_type=F32)


def split(x):
    high = x.astype(BF16)
    return high, (x - high.astype(F32)).astype(BF16)


def dot3(a, b):
    (ah, al), (bh, bl) = a, b
    return dot1(ah, bh) + (dot1(ah, bl) + dot1(al, bh))


def dot_full(a, b):
    return lax.dot_general(
        a, b, (((1,), (0,)), ((), ())), precision=lax.Precision.HIGHEST, preferred_element_type=F32
    )


def eye_mask(n):
    return lax.broadcasted_iota(jnp.int32, (n, n), 0) == lax.broadcasted_iota(jnp.int32, (n, n), 1)


def to_column(row, eye):
    return jnp.sum(jnp.where(eye, row, 0.0), axis=1, keepdims=True)


def invert(x_ref, q_rows, slots, r_ref, q_ref, bh_ref, bl_ref):
    n = x_ref.shape[0]
    b_ref = slots.at[0]
    eye = eye_mask(n)
    one = jnp.where(eye, 1.0, 0.0).astype(F32)
    b = b_ref[...]
    picked = jnp.where(eye, b, 0.0)
    s_row = lax.rsqrt(jnp.sum(picked, axis=0, keepdims=True))
    s_col = lax.rsqrt(jnp.sum(picked, axis=1, keepdims=True))
    b = b * s_row * s_col
    b_ref[...] = b
    high, low = split(b)
    bh_ref[...] = high
    bl_ref[...] = low
    x_ref[...] = one - b
    r0 = x_ref[...].astype(BF16)
    square = dot1(r0, r0)
    r_ref[...] = square.astype(BF16)
    fourth = dot1(r_ref[...], r_ref[...])
    well = jnp.sum(fourth * fourth) < 0.9
    q_ref[...] = fourth.astype(BF16)

    @pl.when(well)
    def _():
        x_ref[...] += jnp.where(eye_mask(n), 1.0, 0.0)
        x_ref[...] += dot1(x_ref[...].astype(BF16), r_ref[...])
        x_ref[...] += dot1(x_ref[...].astype(BF16), q_ref[...])

        def step(carry):
            count, _ = carry
            residual = jnp.where(eye_mask(n), 1.0, 0.0) - dot3(
                (bh_ref[...], bl_ref[...]), split(x_ref[...])
            )
            r_ref[...] = residual.astype(BF16)
            x_ref[...] += dot1(x_ref[...].astype(BF16), r_ref[...])
            return count + 1, jnp.sum(residual * residual)

        lax.while_loop(
            lambda carry: jnp.logical_and(carry[0] < 12, carry[1] > 4e-5),
            step,
            (jnp.int32(0), jnp.float32(1.0)),
        )

    @pl.when(jnp.logical_not(well))
    def _():
        def rows_of(i, size=PART):
            return pl.ds(pl.multiple_of(i * size, size), size)

        def ones_of(i):
            spot = lax.broadcasted_iota(jnp.int32, (PART, n), 0) + i * PART
            return jnp.where(spot == lax.broadcasted_iota(jnp.int32, (PART, n), 1), 1.0, 0.0)

        def widest(i, largest):
            return jnp.maximum(largest, jnp.max(jnp.sum(jnp.abs(slots[0, rows_of(i), :]), axis=1, keepdims=True)))

        alpha = 2.0 / (1.0 + lax.fori_loop(0, n // PART, widest, jnp.float32(1.0)))

        def start(i, _):
            slots[1, rows_of(i), :] = alpha * ones_of(i)
            return 0

        lax.fori_loop(0, n // PART, start, 0)

        def phase(number, total):
            first, second = number // (n // PART), number % (n // PART)
            row = rows_of(second)
            pl.when(first == 0)(lambda: slots.__setitem__((2, row, slice(None)), ones_of(second)))
            q_rows[...] = slots[first, row, :]
            sign = (2 * first - 1).astype(F32)

            def add(k, _):
                slots[2 - first, row, :] += sign * dot_full(
                    q_rows[:, rows_of(k, STEP)], slots[1 + first, rows_of(k, STEP), :]
                )
                return 0

            lax.fori_loop(0, n // STEP, add, 0)
            return total + jnp.where(first == 0, jnp.sum(slots[2, row, :] * slots[2, row, :]), 0.0)

        lax.while_loop(
            lambda carry: jnp.logical_and(carry[0] < 60, carry[1] > 1e-7),
            lambda carry: (carry[0] + 1, lax.fori_loop(0, 2 * (n // PART), phase, jnp.float32(0.0))),
            (jnp.int32(0), jnp.float32(1.0)),
        )

        def finish(i, _):
            x_ref[rows_of(i), :] = slots[1, rows_of(i), :]
            return 0

        lax.fori_loop(0, n // PART, finish, 0)

    x_ref[...] = x_ref[...] * s_row * s_col


STEP = 128
PART = 64
GRAIN = 1.0 / 128.0
FULL = 32767.0
FINE = 4194304.0
SHIFT = 13000.0
MATRIX = ((0, 80, ((384, 4), (0, 1))), (5, 81, ((256, 3), (128, 2))))
SIDE = ((0, 128, ((0, 4), (128, 4), (256, 4), (384, 4))),)
MATRIX_MSG = (82, 16, 128)
SIDE_MSG = (129, 16, 128)


def power_of(size):
    return jnp.ceil(jnp.log2(jnp.maximum(size, 1e-30)) * STEP)


def to_tiles(value):
    return jnp.clip(jnp.round(value), -FULL, FULL).astype(jnp.int32).astype(jnp.int16)


def encode(msg, plan, piece_of):
    lane = lax.broadcasted_iota(jnp.int32, (STEP, STEP), 1)
    eye = eye_mask(STEP)
    for first, spot, pieces in plan:
        scales = jnp.zeros((STEP, STEP), F32)
        place = 8 * first
        for number, (row, wide) in enumerate(pieces):
            piece = piece_of(row, wide * STEP)
            blocks = [piece[:, i * STEP : i * STEP + STEP] for i in range(wide)]
            if plan is MATRIX:
                own = jnp.sum(jnp.where(eye, blocks[-1], 0.0), axis=1, keepdims=True)
                blocks[-1] = jnp.where(eye, 0.0, blocks[-1])
                power = power_of(jnp.abs(own))
                fine = (own * jnp.exp2(power * (-GRAIN)) - 1.0) * FINE
                scales = jnp.where(lane == 4 + number, power + SHIFT, scales)
                scales = jnp.where(lane == 6 + number, fine, scales)
            size = functools.reduce(jnp.maximum, [jnp.abs(block) for block in blocks])
            power = power_of(jnp.max(size, axis=1, keepdims=True))
            unit = jnp.exp2(power * (-GRAIN)) * FULL
            scales = jnp.where(lane == number, power + SHIFT, scales)
            for block in blocks:
                msg[place : place + 8] = to_tiles(block * unit).reshape(8, 16, STEP)
                place += 8
        msg[spot] = to_tiles(scales.T[0:16, :])


def encode_ref(msg, plan, ref):
    encode(msg, plan, lambda row, width: ref[row : row + STEP, 0:width])


def decode(msg, plan):
    eye = eye_mask(STEP)
    for first, spot, pieces in plan:
        flat = msg[spot].astype(jnp.int32).astype(F32)
        codes = jnp.concatenate([flat, jnp.zeros((STEP - 16, STEP), F32)], axis=0).T
        powers = jnp.exp2((codes - SHIFT) * GRAIN)
        place = 8 * first
        for number, (row, wide) in enumerate(pieces):
            unit = powers[:, number : number + 1] * (1.0 / FULL)
            blocks = []
            for _ in range(wide):
                blocks.append(msg[place : place + 8].reshape(STEP, STEP).astype(jnp.int32).astype(F32) * unit)
                place += 8
            if plan is MATRIX:
                own = powers[:, 4 + number : 5 + number] * (1.0 + codes[:, 6 + number : 7 + number] * (1.0 / FINE))
                blocks[-1] = jnp.where(eye, own, blocks[-1])
            yield row, wide * STEP, jnp.concatenate(blocks, axis=1)


def unpack(msgs, plan, target):
    for pieces in zip(*(decode(msg, plan) for msg in msgs)):
        row, width, _ = pieces[0]
        target[row : row + STEP, 0:width] = functools.reduce(lambda p, q: p + q, [piece[2] for piece in pieces])
    if plan is MATRIX:
        for i in range(4):
            for j in range(i):
                target[j * STEP : j * STEP + STEP, i * STEP : i * STEP + STEP] = target[
                    i * STEP : i * STEP + STEP, j * STEP : j * STEP + STEP
                ].T


def scratch_of(n):
    return [
        pltpu.VMEM((PART, n), F32),
        pltpu.VMEM((3, n, n), F32),
        pltpu.VMEM((n, n), BF16),
        pltpu.VMEM((n, n), BF16),
        pltpu.VMEM((n, n), BF16),
        pltpu.VMEM((n, n), BF16),
    ]


def masked(slot, row_interval, turned):
    pick = jnp.where(row_interval[...] == slot, 1.0, 0.0).astype(BF16)
    return turned[...] * pick


ROUNDS = (3, 2, 1, 0)


def each_round(base, place, row_interval, turned, plan, other, msgs, buf, sems):
    def out(i):
        return pltpu.make_async_copy(buf.at[i], msgs[i], sems.at[i])

    def one(i, _):
        left = masked(place[0] ^ (base - i), row_interval, turned)
        encode(buf.at[i], plan, lambda row, width: dot1(left[row : row + STEP, :], other[:, 0:width]))
        for j in range(len(msgs)):
            pl.when(i == j)(lambda: out(j).start())
        return 0

    lax.fori_loop(0, len(msgs), one, 0)
    for j in range(len(msgs)):
        out(j).wait()


def gram_matrix(place, row_interval, design, turned, *rest):
    turned[...] = design[...].T
    each_round(3, place, row_interval, turned, MATRIX, design, rest[:-2], *rest[-2:])


def gram_side(base, place, row_interval, turned, observed, *rest):
    each_round(base, place, row_interval, turned, SIDE, observed, rest[:-2], *rest[-2:])


def first_matrix(one, two, three, four, vec, b_out, x_out, msg, q_rows, slots, r_ref, q_ref, bh, bl):
    b_ref = slots.at[0]
    n = b_out.shape[0]
    unpack((one, two, three, four), MATRIX, b_ref)
    b_ref[...] += jnp.where(eye_mask(n), vec[0:1, :] + vec[1:2, :] + vec[2:3, :], 0.0)
    b_out[...] = b_ref[...]
    invert(x_out, q_rows, slots, r_ref, q_ref, bh, bl)
    encode_ref(msg, MATRIX, x_out)


def first_side(x, one, two, three, four, f_out, msg, t_ref):
    unpack((one, two, three, four), SIDE, f_out)
    t_ref[...] = dot3(split(x[...]), split(f_out[...]))
    encode_ref(msg, SIDE, t_ref)


def second_matrix(b, low, high, vec, b_out, x_out, up, down, q_rows, slots, r_ref, q_ref, bh, bl):
    b_ref = slots.at[0]
    n = b.shape[0]
    eye = eye_mask(n)
    left, right = vec[1:2, :], vec[2:3, :]
    left_col, right_col = to_column(left, eye), to_column(right, eye)
    unpack((low,), MATRIX, b_ref)
    b_out[...] = b[...] - (left_col * b_ref[...]) * left
    unpack((high,), MATRIX, b_ref)
    b_out[...] -= (right_col * b_ref[...]) * right
    b_ref[...] = b_out[...]
    invert(x_out, q_rows, slots, r_ref, q_ref, bh, bl)
    b_ref[...] = (right_col * x_out[...]) * right
    encode_ref(up, MATRIX, b_ref)
    b_ref[...] = (left_col * x_out[...]) * left
    encode_ref(down, MATRIX, b_ref)


def second_side(x, f, low, high, vec, f_out, up, down, t_ref):
    eye = eye_mask(f.shape[0])
    left_col, right_col = to_column(vec[1:2, :], eye), to_column(vec[2:3, :], eye)
    unpack((low,), SIDE, t_ref)
    f_out[...] = f[...] + left_col * t_ref[...]
    unpack((high,), SIDE, t_ref)
    f_out[...] += right_col * t_ref[...]
    value = dot3(split(x[...]), split(f_out[...]))
    t_ref[...] = right_col * value
    encode_ref(up, SIDE, t_ref)
    t_ref[...] = left_col * value
    encode_ref(down, SIDE, t_ref)


def third_matrix(b, low, high, far_low, far_high, vec, x_out, g_ref, h_ref, q_rows, slots, r_ref, q_ref, bh, bl):
    b_ref = slots.at[0]
    n = b.shape[0]
    eye = eye_mask(n)
    b_ref[...] = b[...]
    for near, far, link in ((low, far_low, vec[1:2, :]), (high, far_high, vec[2:3, :])):
        unpack((near,), MATRIX, g_ref)
        unpack((far,), MATRIX, h_ref)
        g = split(g_ref[...])
        half = dot3(g, split(h_ref[...]))
        b_ref[...] -= (to_column(link, eye) * dot3(split(half), g)) * link
    invert(x_out, q_rows, slots, r_ref, q_ref, bh, bl)


def third_side(x, f, low, high, far_low, far_high, vec, msg, out16, g_ref, t_ref, s_ref):
    eye = eye_mask(f.shape[0])
    s_ref[...] = f[...]
    for near, far, link in ((low, far_low, vec[1:2, :]), (high, far_high, vec[2:3, :])):
        unpack((near,), MATRIX, g_ref)
        unpack((far,), SIDE, t_ref)
        s_ref[...] += to_column(link, eye) * dot3(split(g_ref[...]), split(t_ref[...]))
    t_ref[...] = dot3(split(x[...]), split(s_ref[...]))
    encode_ref(msg, SIDE, t_ref)
    out16[...] = t_ref[...].astype(BF16)


def arrive(msg, out, out16):
    unpack((msg,), SIDE, out)
    out16[...] = out[...].astype(BF16)


def call(kernel, outs, scratch, *args):
    return pl.pallas_call(kernel, out_shape=outs, scratch_shapes=scratch)(*args)


def gram(kernel, kept, msgs, place, *args):
    space = pl.BlockSpec(memory_space=pltpu.VMEM)
    specs = [pl.BlockSpec(memory_space=pltpu.SMEM)] + [space] * len(args)
    return pl.pallas_call(
        kernel,
        out_shape=kept + msgs,
        in_specs=specs,
        out_specs=(space,) * len(kept) + (pl.BlockSpec(memory_space=pl.ANY),) * len(msgs),
        scratch_shapes=[
            pltpu.VMEM((len(msgs),) + msgs[0].shape, jnp.int16),
            pltpu.SemaphoreType.DMA((len(msgs),)),
        ],
    )(place, *args)


def step_of(design, observed, row_interval, prior_ridge, coupling):
    row_count, n = design.shape
    count = lax.axis_size(PAIR)
    chain, place = lax.axis_index("chain"), lax.axis_index("arc")
    time = LINE * (chain // 2) + 2 * place + chain % 2
    square = jax.ShapeDtypeStruct((n, n), F32)
    half = jax.ShapeDtypeStruct((n, n), BF16)
    matrix_msg = jax.ShapeDtypeStruct(MATRIX_MSG, jnp.int16)
    side_msg = jax.ShapeDtypeStruct(SIDE_MSG, jnp.int16)
    flat = row_interval.reshape(1, row_count)
    where = place.astype(jnp.int32).reshape(1)
    plain = [pltpu.VMEM((n, n), F32)]
    work = scratch_of(n)

    turned, *parts = gram(
        gram_matrix, (jax.ShapeDtypeStruct((n, row_count), BF16),), (matrix_msg,) * 4, where, flat, design
    )
    for i, m in enumerate(ROUNDS):
        parts[i] = to_seat(parts[i], m)
    side_parts = []
    for i in (0, 2):
        rounds = ROUNDS[i : i + 2]
        msgs = gram(functools.partial(gram_side, 3 - i), (), (side_msg,) * 2, where, flat, turned, observed)
        for j, m in enumerate(rounds):
            side_parts.append(to_seat(msgs[j], m))
    mine = carry(jnp.concatenate([prior_ridge, coupling], axis=0), home, seat)
    left_link = carry(coupling, home, lambda t: seat(t + 1) if t + 1 < count else None)
    right_link = jnp.where(time == count - 1, 0.0, mine[1:2])
    vec = jnp.concatenate([mine[0:1], left_link, right_link, jnp.zeros((5, n), F32)], axis=0)
    block, inverse, near = call(first_matrix, (square, square, matrix_msg), work, *parts, vec)
    low, high = along(near, 1), along(near, -1)
    side, near_side = call(first_side, (square, side_msg), plain, inverse, *side_parts)
    low_side, high_side = along(near_side, 1), along(near_side, -1)
    block_one, inverse_one, up, down = call(
        second_matrix, (square, square, matrix_msg, matrix_msg), work, block, low, high, vec
    )
    far_low, far_high = along(up, 2), along(down, -2)
    side_one, up_side, down_side = call(
        second_side, (square, side_msg, side_msg), plain, inverse_one, side, low_side, high_side, vec
    )
    far_low_side, far_high_side = along(up_side, 2), along(down_side, -2)
    inverse_two = call(third_matrix, square, plain * 2 + work, block_one, low, high, far_low, far_high, vec)
    code, rounded = call(
        third_side, (side_msg, half), plain * 3, inverse_two, side_one, low, high, far_low_side, far_high_side, vec
    )
    states = []
    for m in range(SLOTS):
        states.append(to_arc(rounded if m else code, m))
    solution, states[0] = call(arrive, (square, half), [], states[0])
    residual = observed.astype(F32)
    for m in range(SLOTS):
        picked = jnp.where((row_interval == (place ^ m))[:, None], design, jnp.zeros((), design.dtype))
        residual = residual - jnp.dot(picked, states[m], preferred_element_type=F32)
    return (solution[None], residual)


def solution(mesh):
    placed = (P(PAIR, None), P(PAIR, None), P(PAIR), P(PAIR, None), P(PAIR, None))
    return jax.shard_map(
        step_of,
        mesh=mesh,
        in_specs=placed,
        out_specs=(P(PAIR, None, None), P(PAIR, None)),
        check_vma=False,
    )
```

```python
import functools

import jax
import jax.numpy as jnp
from jax import lax
from jax.experimental import pallas as pl
from jax.experimental.pallas import tpu as pltpu
from jax.sharding import PartitionSpec as P

F32 = jnp.float32
BF16 = jnp.bfloat16
PAIR = ("chain", "arc")


SLOTS = 4
LINE = 2 * SLOTS


def seat(t):
    line, spot = t // LINE, t % LINE
    return (2 * line + spot % 2) * SLOTS + spot // 2


def carry(value, source_of, target_of):
    count = lax.axis_size(PAIR)
    pairs = [(source_of(t), target_of(t)) for t in range(count)]
    return lax.ppermute(value, PAIR, [pair for pair in pairs if pair[1] is not None])


def along(value, steps):
    count = lax.axis_size(PAIR)
    return carry(value, seat, lambda t: seat(t + steps) if 0 <= t + steps < count else None)


def home(t):
    return t


def to_seat(value, m):
    return carry(value, lambda t: t - t % SLOTS + (t % SLOTS ^ m), seat)


def to_arc(value, m):
    return carry(value, seat, lambda t: t - t % SLOTS + (t % SLOTS ^ m))


def dot1(a, b):
    return lax.dot_general(a, b, (((1,), (0,)), ((), ())), preferred_element_type=F32)


def split(x):
    high = x.astype(BF16)
    return high, (x - high.astype(F32)).astype(BF16)


def dot3(a, b):
    (ah, al), (bh, bl) = a, b
    return dot1(ah, bh) + (dot1(ah, bl) + dot1(al, bh))


def dot_full(a, b):
    return lax.dot_general(
        a, b, (((1,), (0,)), ((), ())), precision=lax.Precision.HIGHEST, preferred_element_type=F32
    )


def eye_mask(n):
    return lax.broadcasted_iota(jnp.int32, (n, n), 0) == lax.broadcasted_iota(jnp.int32, (n, n), 1)


def to_column(row, eye):
    return jnp.sum(jnp.where(eye, row, 0.0), axis=1, keepdims=True)


def invert(x_ref, q_rows, slots, r_ref, q_ref, bh_ref, bl_ref):
    n = x_ref.shape[0]
    b_ref = slots.at[0]
    eye = eye_mask(n)
    one = jnp.where(eye, 1.0, 0.0).astype(F32)
    b = b_ref[...]
    picked = jnp.where(eye, b, 0.0)
    s_row = lax.rsqrt(jnp.sum(picked, axis=0, keepdims=True))
    s_col = lax.rsqrt(jnp.sum(picked, axis=1, keepdims=True))
    b = b * s_row * s_col
    b_ref[...] = b
    high, low = split(b)
    bh_ref[...] = high
    bl_ref[...] = low
    x_ref[...] = one - b
    r0 = x_ref[...].astype(BF16)
    square = dot1(r0, r0)
    r_ref[...] = square.astype(BF16)
    fourth = dot1(r_ref[...], r_ref[...])
    well = jnp.sum(fourth * fourth) < 0.9
    q_ref[...] = fourth.astype(BF16)

    @pl.when(well)
    def _():
        x_ref[...] += jnp.where(eye_mask(n), 1.0, 0.0)
        x_ref[...] += dot1(x_ref[...].astype(BF16), r_ref[...])
        x_ref[...] += dot1(x_ref[...].astype(BF16), q_ref[...])

        def step(carry):
            count, _ = carry
            residual = jnp.where(eye_mask(n), 1.0, 0.0) - dot3(
                (bh_ref[...], bl_ref[...]), split(x_ref[...])
            )
            r_ref[...] = residual.astype(BF16)
            x_ref[...] += dot1(x_ref[...].astype(BF16), r_ref[...])
            return count + 1, jnp.sum(residual * residual)

        lax.while_loop(
            lambda carry: jnp.logical_and(carry[0] < 12, carry[1] > 4e-5),
            step,
            (jnp.int32(0), jnp.float32(1.0)),
        )

    @pl.when(jnp.logical_not(well))
    def _():
        def rows_of(i, size=PART):
            return pl.ds(pl.multiple_of(i * size, size), size)

        def ones_of(i):
            spot = lax.broadcasted_iota(jnp.int32, (PART, n), 0) + i * PART
            return jnp.where(spot == lax.broadcasted_iota(jnp.int32, (PART, n), 1), 1.0, 0.0)

        def widest(i, largest):
            return jnp.maximum(largest, jnp.max(jnp.sum(jnp.abs(slots[0, rows_of(i), :]), axis=1, keepdims=True)))

        alpha = 2.0 / (1.0 + lax.fori_loop(0, n // PART, widest, jnp.float32(1.0)))

        def start(i, _):
            slots[1, rows_of(i), :] = alpha * ones_of(i)
            return 0

        lax.fori_loop(0, n // PART, start, 0)

        def phase(number, total):
            first, second = number // (n // PART), number % (n // PART)
            row = rows_of(second)
            pl.when(first == 0)(lambda: slots.__setitem__((2, row, slice(None)), ones_of(second)))
            q_rows[...] = slots[first, row, :]
            sign = (2 * first - 1).astype(F32)

            def add(k, _):
                slots[2 - first, row, :] += sign * dot_full(
                    q_rows[:, rows_of(k, STEP)], slots[1 + first, rows_of(k, STEP), :]
                )
                return 0

            lax.fori_loop(0, n // STEP, add, 0)
            return total + jnp.where(first == 0, jnp.sum(slots[2, row, :] * slots[2, row, :]), 0.0)

        lax.while_loop(
            lambda carry: jnp.logical_and(carry[0] < 60, carry[1] > 1e-7),
            lambda carry: (carry[0] + 1, lax.fori_loop(0, 2 * (n // PART), phase, jnp.float32(0.0))),
            (jnp.int32(0), jnp.float32(1.0)),
        )

        def finish(i, _):
            x_ref[rows_of(i), :] = slots[1, rows_of(i), :]
            return 0

        lax.fori_loop(0, n // PART, finish, 0)

    x_ref[...] = x_ref[...] * s_row * s_col


STEP = 128
PART = 64
GRAIN = 1.0 / 128.0
FULL = 32767.0
FINE = 4194304.0
SHIFT = 13000.0
MATRIX = ((0, 80, ((384, 4), (0, 1))), (5, 81, ((256, 3), (128, 2))))
SIDE = ((0, 128, ((0, 4), (128, 4), (256, 4), (384, 4))),)
MATRIX_MSG = (82, 16, 128)
SIDE_MSG = (129, 16, 128)


def power_of(size):
    return jnp.ceil(jnp.log2(jnp.maximum(size, 1e-30)) * STEP)


def to_tiles(value):
    return jnp.clip(jnp.round(value), -FULL, FULL).astype(jnp.int32).astype(jnp.int16)


def encode(msg, plan, piece_of):
    lane = lax.broadcasted_iota(jnp.int32, (STEP, STEP), 1)
    eye = eye_mask(STEP)
    for first, spot, pieces in plan:
        scales = jnp.zeros((STEP, STEP), F32)
        place = 8 * first
        for number, (row, wide) in enumerate(pieces):
            piece = piece_of(row, wide * STEP)
            blocks = [piece[:, i * STEP : i * STEP + STEP] for i in range(wide)]
            if plan is MATRIX:
                own = jnp.sum(jnp.where(eye, blocks[-1], 0.0), axis=1, keepdims=True)
                blocks[-1] = jnp.where(eye, 0.0, blocks[-1])
                power = power_of(jnp.abs(own))
                fine = (own * jnp.exp2(power * (-GRAIN)) - 1.0) * FINE
                scales = jnp.where(lane == 4 + number, power + SHIFT, scales)
                scales = jnp.where(lane == 6 + number, fine, scales)
            size = functools.reduce(jnp.maximum, [jnp.abs(block) for block in blocks])
            power = power_of(jnp.max(size, axis=1, keepdims=True))
            unit = jnp.exp2(power * (-GRAIN)) * FULL
            scales = jnp.where(lane == number, power + SHIFT, scales)
            for block in blocks:
                msg[place : place + 8] = to_tiles(block * unit).reshape(8, 16, STEP)
                place += 8
        msg[spot] = to_tiles(scales.T[0:16, :])


def encode_ref(msg, plan, ref):
    encode(msg, plan, lambda row, width: ref[row : row + STEP, 0:width])


def decode(msg, plan):
    eye = eye_mask(STEP)
    for first, spot, pieces in plan:
        flat = msg[spot].astype(jnp.int32).astype(F32)
        codes = jnp.concatenate([flat, jnp.zeros((STEP - 16, STEP), F32)], axis=0).T
        powers = jnp.exp2((codes - SHIFT) * GRAIN)
        place = 8 * first
        for number, (row, wide) in enumerate(pieces):
            unit = powers[:, number : number + 1] * (1.0 / FULL)
            blocks = []
            for _ in range(wide):
                blocks.append(msg[place : place + 8].reshape(STEP, STEP).astype(jnp.int32).astype(F32) * unit)
                place += 8
            if plan is MATRIX:
                own = powers[:, 4 + number : 5 + number] * (1.0 + codes[:, 6 + number : 7 + number] * (1.0 / FINE))
                blocks[-1] = jnp.where(eye, own, blocks[-1])
            yield row, wide * STEP, jnp.concatenate(blocks, axis=1)


def unpack(msgs, plan, target):
    for pieces in zip(*(decode(msg, plan) for msg in msgs)):
        row, width, _ = pieces[0]
        target[row : row + STEP, 0:width] = functools.reduce(lambda p, q: p + q, [piece[2] for piece in pieces])
    if plan is MATRIX:
        for i in range(4):
            for j in range(i):
                target[j * STEP : j * STEP + STEP, i * STEP : i * STEP + STEP] = target[
                    i * STEP : i * STEP + STEP, j * STEP : j * STEP + STEP
                ].T


def scratch_of(n):
    return [
        pltpu.VMEM((PART, n), F32),
        pltpu.VMEM((3, n, n), F32),
        pltpu.VMEM((n, n), BF16),
        pltpu.VMEM((n, n), BF16),
        pltpu.VMEM((n, n), BF16),
        pltpu.VMEM((n, n), BF16),
    ]


def masked(slot, row_interval, turned):
    pick = jnp.where(row_interval[...] == slot, 1.0, 0.0).astype(BF16)
    return turned[...] * pick


ROUNDS = (3, 2, 1, 0)


def each_round(base, place, row_interval, turned, plan, other, msgs, buf, sems):
    def out(i):
        return pltpu.make_async_copy(buf.at[i], msgs[i], sems.at[i])

    def one(i, _):
        left = masked(place[0] ^ (base - i), row_interval, turned)
        encode(buf.at[i], plan, lambda row, width: dot1(left[row : row + STEP, :], other[:, 0:width]))
        for j in range(len(msgs)):
            pl.when(i == j)(lambda: out(j).start())
        return 0

    lax.fori_loop(0, len(msgs), one, 0, unroll=2 if plan is MATRIX else 1)
    for j in range(len(msgs)):
        out(j).wait()


def gram_matrix(place, row_interval, design, turned, *rest):
    turned[...] = design[...].T
    each_round(3, place, row_interval, turned, MATRIX, design, rest[:-2], *rest[-2:])


def gram_side(base, place, row_interval, turned, observed, *rest):
    each_round(base, place, row_interval, turned, SIDE, observed, rest[:-2], *rest[-2:])


def first_matrix(one, two, three, four, vec, b_out, x_out, msg, q_rows, slots, r_ref, q_ref, bh, bl):
    b_ref = slots.at[0]
    n = b_out.shape[0]
    unpack((one, two, three, four), MATRIX, b_ref)
    b_ref[...] += jnp.where(eye_mask(n), vec[0:1, :] + vec[1:2, :] + vec[2:3, :], 0.0)
    b_out[...] = b_ref[...]
    invert(x_out, q_rows, slots, r_ref, q_ref, bh, bl)
    encode_ref(msg, MATRIX, x_out)


def first_side(x, one, two, three, four, f_out, msg, t_ref):
    unpack((one, two, three, four), SIDE, f_out)
    t_ref[...] = dot3(split(x[...]), split(f_out[...]))
    encode_ref(msg, SIDE, t_ref)


def second_matrix(b, low, high, vec, b_out, x_out, up, down, q_rows, slots, r_ref, q_ref, bh, bl):
    b_ref = slots.at[0]
    n = b.shape[0]
    eye = eye_mask(n)
    left, right = vec[1:2, :], vec[2:3, :]
    left_col, right_col = to_column(left, eye), to_column(right, eye)
    unpack((low,), MATRIX, b_ref)
    b_out[...] = b[...] - (left_col * b_ref[...]) * left
    unpack((high,), MATRIX, b_ref)
    b_out[...] -= (right_col * b_ref[...]) * right
    b_ref[...] = b_out[...]
    invert(x_out, q_rows, slots, r_ref, q_ref, bh, bl)
    b_ref[...] = (right_col * x_out[...]) * right
    encode_ref(up, MATRIX, b_ref)
    b_ref[...] = (left_col * x_out[...]) * left
    encode_ref(down, MATRIX, b_ref)


def second_side(x, f, low, high, vec, f_out, up, down, t_ref):
    eye = eye_mask(f.shape[0])
    left_col, right_col = to_column(vec[1:2, :], eye), to_column(vec[2:3, :], eye)
    unpack((low,), SIDE, t_ref)
    f_out[...] = f[...] + left_col * t_ref[...]
    unpack((high,), SIDE, t_ref)
    f_out[...] += right_col * t_ref[...]
    value = dot3(split(x[...]), split(f_out[...]))
    t_ref[...] = right_col * value
    encode_ref(up, SIDE, t_ref)
    t_ref[...] = left_col * value
    encode_ref(down, SIDE, t_ref)


def third_matrix(b, low, high, far_low, far_high, vec, x_out, g_ref, h_ref, q_rows, slots, r_ref, q_ref, bh, bl):
    b_ref = slots.at[0]
    n = b.shape[0]
    eye = eye_mask(n)
    b_ref[...] = b[...]
    for near, far, link in ((low, far_low, vec[1:2, :]), (high, far_high, vec[2:3, :])):
        unpack((near,), MATRIX, g_ref)
        unpack((far,), MATRIX, h_ref)
        g = split(g_ref[...])
        half = dot3(g, split(h_ref[...]))
        b_ref[...] -= (to_column(link, eye) * dot3(split(half), g)) * link
    invert(x_out, q_rows, slots, r_ref, q_ref, bh, bl)


def third_side(x, f, low, high, far_low, far_high, vec, msg, out16, g_ref, t_ref, s_ref):
    eye = eye_mask(f.shape[0])
    s_ref[...] = f[...]
    for near, far, link in ((low, far_low, vec[1:2, :]), (high, far_high, vec[2:3, :])):
        unpack((near,), MATRIX, g_ref)
        unpack((far,), SIDE, t_ref)
        s_ref[...] += to_column(link, eye) * dot3(split(g_ref[...]), split(t_ref[...]))
    t_ref[...] = dot3(split(x[...]), split(s_ref[...]))
    encode_ref(msg, SIDE, t_ref)
    out16[...] = t_ref[...].astype(BF16)


def predict(place, column, design, partial, code, two, three, out, residual, x_ref):
    n = out.shape[0]

    @pl.when(pl.program_id(0) == 0)
    def _():
        unpack((code,), SIDE, out)
        x_ref[0:n, :] = out[...].astype(BF16)
        x_ref[n : 2 * n, :] = two[...]
        x_ref[2 * n : 3 * n, :] = three[...]

    d = design[...]
    picked = []
    for m in (0, 2, 3):
        pick = jnp.where(column[...] == (place[0] ^ m), 1.0, 0.0)
        pick = jnp.broadcast_to(pick, (d.shape[0], STEP)).astype(BF16)
        picked.append(d * jnp.concatenate([pick] * (n // STEP), axis=1))
    residual[...] = partial[...] - dot1(jnp.concatenate(picked, axis=1), x_ref[...])


def call(kernel, outs, scratch, *args):
    return pl.pallas_call(kernel, out_shape=outs, scratch_shapes=scratch)(*args)


def gram(kernel, kept, msgs, place, *args):
    space = pl.BlockSpec(memory_space=pltpu.VMEM)
    specs = [pl.BlockSpec(memory_space=pltpu.SMEM)] + [space] * len(args)
    return pl.pallas_call(
        kernel,
        out_shape=kept + msgs,
        in_specs=specs,
        out_specs=(space,) * len(kept) + (pl.BlockSpec(memory_space=pl.ANY),) * len(msgs),
        scratch_shapes=[
            pltpu.VMEM((len(msgs),) + msgs[0].shape, jnp.int16),
            pltpu.SemaphoreType.DMA((len(msgs),)),
        ],
    )(place, *args)


def step_of(design, observed, row_interval, prior_ridge, coupling):
    row_count, n = design.shape
    count = lax.axis_size(PAIR)
    chain, place = lax.axis_index("chain"), lax.axis_index("arc")
    time = LINE * (chain // 2) + 2 * place + chain % 2
    square = jax.ShapeDtypeStruct((n, n), F32)
    half = jax.ShapeDtypeStruct((n, n), BF16)
    matrix_msg = jax.ShapeDtypeStruct(MATRIX_MSG, jnp.int16)
    side_msg = jax.ShapeDtypeStruct(SIDE_MSG, jnp.int16)
    flat = row_interval.reshape(1, row_count)
    where = place.astype(jnp.int32).reshape(1)
    plain = [pltpu.VMEM((n, n), F32)]
    work = scratch_of(n)

    turned, *parts = gram(
        gram_matrix, (jax.ShapeDtypeStruct((n, row_count), BF16),), (matrix_msg,) * 4, where, flat, design
    )
    for i, m in enumerate(ROUNDS):
        parts[i] = to_seat(parts[i], m)
    side_parts = []
    for i in (0, 2):
        rounds = ROUNDS[i : i + 2]
        msgs = gram(functools.partial(gram_side, 3 - i), (), (side_msg,) * 2, where, flat, turned, observed)
        for j, m in enumerate(rounds):
            side_parts.append(to_seat(msgs[j], m))
    mine = carry(jnp.concatenate([prior_ridge, coupling], axis=0), home, seat)
    left_link = carry(coupling, home, lambda t: seat(t + 1) if t + 1 < count else None)
    right_link = jnp.where(time == count - 1, 0.0, mine[1:2])
    vec = jnp.concatenate([mine[0:1], left_link, right_link, jnp.zeros((5, n), F32)], axis=0)
    block, inverse, near = call(first_matrix, (square, square, matrix_msg), work, *parts, vec)
    low, high = along(near, 1), along(near, -1)
    side, near_side = call(first_side, (square, side_msg), plain, inverse, *side_parts)
    low_side, high_side = along(near_side, 1), along(near_side, -1)
    block_one, inverse_one, up, down = call(
        second_matrix, (square, square, matrix_msg, matrix_msg), work, block, low, high, vec
    )
    far_low, far_high = along(up, 2), along(down, -2)
    side_one, up_side, down_side = call(
        second_side, (square, side_msg, side_msg), plain, inverse_one, side, low_side, high_side, vec
    )
    far_low_side, far_high_side = along(up_side, 2), along(down_side, -2)
    inverse_two = call(third_matrix, square, plain * 2 + work, block_one, low, high, far_low, far_high, vec)
    code, rounded = call(
        third_side, (side_msg, half), plain * 3, inverse_two, side_one, low, high, far_low_side, far_high_side, vec
    )
    states = []
    for m in range(SLOTS):
        states.append(to_arc(rounded if m else code, m))
    picked = jnp.where((row_interval == (place ^ 1))[:, None], design, jnp.zeros((), design.dtype))
    partial = observed.astype(F32) - jnp.dot(picked, states[1], preferred_element_type=F32)
    chunk = row_count // SLOTS
    whole = pl.BlockSpec(memory_space=pltpu.VMEM)
    rows = lambda width: pl.BlockSpec((chunk, width), lambda i: (i, 0))
    solution, residual = pl.pallas_call(
        predict,
        grid=(SLOTS,),
        out_shape=(square, jax.ShapeDtypeStruct((row_count, n), F32)),
        in_specs=[pl.BlockSpec(memory_space=pltpu.SMEM), rows(1), rows(n), rows(n), whole, whole, whole],
        out_specs=(pl.BlockSpec((n, n), lambda i: (0, 0)), rows(n)),
        scratch_shapes=[pltpu.VMEM((3 * n, n), BF16)],
    )(where, row_interval.reshape(row_count, 1), design, partial, states[0], states[2], states[3])
    return (solution[None], residual)


def solution(mesh):
    placed = (P(PAIR, None), P(PAIR, None), P(PAIR), P(PAIR, None), P(PAIR, None))
    return jax.shard_map(
        step_of,
        mesh=mesh,
        in_specs=placed,
        out_specs=(P(PAIR, None, None), P(PAIR, None)),
        check_vma=False,
    )
```

```python
import functools

import jax
import jax.numpy as jnp
from jax import lax
from jax.experimental import pallas as pl
from jax.experimental.pallas import tpu as pltpu
from jax.sharding import PartitionSpec as P

F32 = jnp.float32
BF16 = jnp.bfloat16
PAIR = ("chain", "arc")


SLOTS = 4
LINE = 2 * SLOTS


def seat(t):
    line, spot = t // LINE, t % LINE
    chip = spot // 2 if line % 2 == 0 else SLOTS - 1 - spot // 2
    return (2 * line + spot % 2) * SLOTS + chip


def carry(value, source_of, target_of):
    count = lax.axis_size(PAIR)
    pairs = [(source_of(t), target_of(t)) for t in range(count)]
    return lax.ppermute(value, PAIR, [pair for pair in pairs if pair[1] is not None])


def along(value, steps):
    count = lax.axis_size(PAIR)
    return carry(value, seat, lambda t: seat(t + steps) if 0 <= t + steps < count else None)


def home(t):
    return t


def to_seat(value, m):
    return carry(value, lambda t: t - t % SLOTS + (t % SLOTS ^ m), seat)


def to_arc(value, m):
    return carry(value, seat, lambda t: t - t % SLOTS + (t % SLOTS ^ m))


def dot1(a, b):
    return lax.dot_general(a, b, (((1,), (0,)), ((), ())), preferred_element_type=F32)


def split(x):
    high = x.astype(BF16)
    return high, (x - high.astype(F32)).astype(BF16)


def dot3(a, b):
    (ah, al), (bh, bl) = a, b
    return dot1(ah, bh) + (dot1(ah, bl) + dot1(al, bh))


def dot_full(a, b):
    return lax.dot_general(
        a, b, (((1,), (0,)), ((), ())), precision=lax.Precision.HIGHEST, preferred_element_type=F32
    )


def eye_mask(n):
    return lax.broadcasted_iota(jnp.int32, (n, n), 0) == lax.broadcasted_iota(jnp.int32, (n, n), 1)


def to_column(row, eye):
    return jnp.sum(jnp.where(eye, row, 0.0), axis=1, keepdims=True)


def invert(x_ref, q_rows, slots, r_ref, q_ref, bh_ref, bl_ref):
    n = x_ref.shape[0]
    b_ref = slots.at[0]
    eye = eye_mask(n)
    one = jnp.where(eye, 1.0, 0.0).astype(F32)
    b = b_ref[...]
    picked = jnp.where(eye, b, 0.0)
    s_row = lax.rsqrt(jnp.sum(picked, axis=0, keepdims=True))
    s_col = lax.rsqrt(jnp.sum(picked, axis=1, keepdims=True))
    b = b * s_row * s_col
    b_ref[...] = b
    high, low = split(b)
    bh_ref[...] = high
    bl_ref[...] = low
    x_ref[...] = one - b
    r0 = x_ref[...].astype(BF16)
    square = dot1(r0, r0)
    r_ref[...] = square.astype(BF16)
    fourth = dot1(r_ref[...], r_ref[...])
    well = jnp.sum(fourth * fourth) < 0.9
    q_ref[...] = fourth.astype(BF16)

    @pl.when(well)
    def _():
        x_ref[...] += jnp.where(eye_mask(n), 1.0, 0.0)
        x_ref[...] += dot1(x_ref[...].astype(BF16), r_ref[...])
        x_ref[...] += dot1(x_ref[...].astype(BF16), q_ref[...])

        def step(carry):
            count, _ = carry
            residual = jnp.where(eye_mask(n), 1.0, 0.0) - dot3(
                (bh_ref[...], bl_ref[...]), split(x_ref[...])
            )
            r_ref[...] = residual.astype(BF16)
            x_ref[...] += dot1(x_ref[...].astype(BF16), r_ref[...])
            return count + 1, jnp.sum(residual * residual)

        lax.while_loop(
            lambda carry: jnp.logical_and(carry[0] < 12, carry[1] > 4e-5),
            step,
            (jnp.int32(0), jnp.float32(1.0)),
        )

    @pl.when(jnp.logical_not(well))
    def _():
        def rows_of(i, size=PART):
            return pl.ds(pl.multiple_of(i * size, size), size)

        def ones_of(i):
            spot = lax.broadcasted_iota(jnp.int32, (PART, n), 0) + i * PART
            return jnp.where(spot == lax.broadcasted_iota(jnp.int32, (PART, n), 1), 1.0, 0.0)

        def widest(i, largest):
            return jnp.maximum(largest, jnp.max(jnp.sum(jnp.abs(slots[0, rows_of(i), :]), axis=1, keepdims=True)))

        alpha = 2.0 / (1.0 + lax.fori_loop(0, n // PART, widest, jnp.float32(1.0)))

        def start(i, _):
            slots[1, rows_of(i), :] = alpha * ones_of(i)
            return 0

        lax.fori_loop(0, n // PART, start, 0)

        def phase(number, total):
            first, second = number // (n // PART), number % (n // PART)
            row = rows_of(second)
            pl.when(first == 0)(lambda: slots.__setitem__((2, row, slice(None)), ones_of(second)))
            q_rows[...] = slots[first, row, :]
            sign = (2 * first - 1).astype(F32)

            def add(k, _):
                slots[2 - first, row, :] += sign * dot_full(
                    q_rows[:, rows_of(k, STEP)], slots[1 + first, rows_of(k, STEP), :]
                )
                return 0

            lax.fori_loop(0, n // STEP, add, 0)
            return total + jnp.where(first == 0, jnp.sum(slots[2, row, :] * slots[2, row, :]), 0.0)

        lax.while_loop(
            lambda carry: jnp.logical_and(carry[0] < 60, carry[1] > 1e-7),
            lambda carry: (carry[0] + 1, lax.fori_loop(0, 2 * (n // PART), phase, jnp.float32(0.0))),
            (jnp.int32(0), jnp.float32(1.0)),
        )

        def finish(i, _):
            x_ref[rows_of(i), :] = slots[1, rows_of(i), :]
            return 0

        lax.fori_loop(0, n // PART, finish, 0)

    x_ref[...] = x_ref[...] * s_row * s_col


STEP = 128
PART = 64
GRAIN = 1.0 / 128.0
FULL = 32767.0
FINE = 4194304.0
SHIFT = 13000.0
MATRIX = ((0, 80, ((384, 4), (0, 1))), (5, 81, ((256, 3), (128, 2))))
SIDE = ((0, 128, ((0, 4), (128, 4), (256, 4), (384, 4))),)
MATRIX_MSG = (82, 16, 128)
SIDE_MSG = (129, 16, 128)


def power_of(size):
    return jnp.ceil(jnp.log2(jnp.maximum(size, 1e-30)) * STEP)


def to_tiles(value):
    return jnp.clip(jnp.round(value), -FULL, FULL).astype(jnp.int32).astype(jnp.int16)


def encode(msg, plan, piece_of):
    lane = lax.broadcasted_iota(jnp.int32, (STEP, STEP), 1)
    eye = eye_mask(STEP)
    for first, spot, pieces in plan:
        scales = jnp.zeros((STEP, STEP), F32)
        place = 8 * first
        for number, (row, wide) in enumerate(pieces):
            piece = piece_of(row, wide * STEP)
            blocks = [piece[:, i * STEP : i * STEP + STEP] for i in range(wide)]
            if plan is MATRIX:
                own = jnp.sum(jnp.where(eye, blocks[-1], 0.0), axis=1, keepdims=True)
                blocks[-1] = jnp.where(eye, 0.0, blocks[-1])
                power = power_of(jnp.abs(own))
                fine = (own * jnp.exp2(power * (-GRAIN)) - 1.0) * FINE
                scales = jnp.where(lane == 4 + number, power + SHIFT, scales)
                scales = jnp.where(lane == 6 + number, fine, scales)
            size = functools.reduce(jnp.maximum, [jnp.abs(block) for block in blocks])
            power = power_of(jnp.max(size, axis=1, keepdims=True))
            unit = jnp.exp2(power * (-GRAIN)) * FULL
            scales = jnp.where(lane == number, power + SHIFT, scales)
            for block in blocks:
                msg[place : place + 8] = to_tiles(block * unit).reshape(8, 16, STEP)
                place += 8
        msg[spot] = to_tiles(scales.T[0:16, :])


def encode_ref(msg, plan, ref):
    encode(msg, plan, lambda row, width: ref[row : row + STEP, 0:width])


def decode(msg, plan):
    eye = eye_mask(STEP)
    for first, spot, pieces in plan:
        flat = msg[spot].astype(jnp.int32).astype(F32)
        codes = jnp.concatenate([flat, jnp.zeros((STEP - 16, STEP), F32)], axis=0).T
        powers = jnp.exp2((codes - SHIFT) * GRAIN)
        place = 8 * first
        for number, (row, wide) in enumerate(pieces):
            unit = powers[:, number : number + 1] * (1.0 / FULL)
            blocks = []
            for _ in range(wide):
                blocks.append(msg[place : place + 8].reshape(STEP, STEP).astype(jnp.int32).astype(F32) * unit)
                place += 8
            if plan is MATRIX:
                own = powers[:, 4 + number : 5 + number] * (1.0 + codes[:, 6 + number : 7 + number] * (1.0 / FINE))
                blocks[-1] = jnp.where(eye, own, blocks[-1])
            yield row, wide * STEP, jnp.concatenate(blocks, axis=1)


def unpack(msgs, plan, target):
    for pieces in zip(*(decode(msg, plan) for msg in msgs)):
        row, width, _ = pieces[0]
        target[row : row + STEP, 0:width] = functools.reduce(lambda p, q: p + q, [piece[2] for piece in pieces])
    if plan is MATRIX:
        for i in range(4):
            for j in range(i):
                target[j * STEP : j * STEP + STEP, i * STEP : i * STEP + STEP] = target[
                    i * STEP : i * STEP + STEP, j * STEP : j * STEP + STEP
                ].T


def scratch_of(n):
    return [
        pltpu.VMEM((PART, n), F32),
        pltpu.VMEM((3, n, n), F32),
        pltpu.VMEM((n, n), BF16),
        pltpu.VMEM((n, n), BF16),
        pltpu.VMEM((n, n), BF16),
        pltpu.VMEM((n, n), BF16),
    ]


def masked(slot, row_interval, turned):
    pick = jnp.where(row_interval[...] == slot, 1.0, 0.0).astype(BF16)
    return turned[...] * pick


ROUNDS = (3, 2, 1, 0)


def each_round(base, place, row_interval, turned, plan, other, msgs, buf, sems):
    def out(i):
        return pltpu.make_async_copy(buf.at[i], msgs[i], sems.at[i])

    def one(i, _):
        left = masked(place[0] ^ (base - i), row_interval, turned)
        encode(buf.at[i], plan, lambda row, width: dot1(left[row : row + STEP, :], other[:, 0:width]))
        for j in range(len(msgs)):
            pl.when(i == j)(lambda: out(j).start())
        return 0

    lax.fori_loop(0, len(msgs), one, 0)
    for j in range(len(msgs)):
        out(j).wait()


def gram_first(base, place, row_interval, design, turned, *rest):
    turned[...] = design[...].T
    each_round(base, place, row_interval, turned, MATRIX, design, rest[:-2], *rest[-2:])


def gram_matrix(base, place, row_interval, turned, design, *rest):
    each_round(base, place, row_interval, turned, MATRIX, design, rest[:-2], *rest[-2:])


def gram_side(base, place, row_interval, turned, observed, *rest):
    each_round(base, place, row_interval, turned, SIDE, observed, rest[:-2], *rest[-2:])


def first_matrix(one, two, three, four, vec, b_out, x_out, msg, q_rows, slots, r_ref, q_ref, bh, bl):
    b_ref = slots.at[0]
    n = b_out.shape[0]
    unpack((one, two, three, four), MATRIX, b_ref)
    b_ref[...] += jnp.where(eye_mask(n), vec[0:1, :] + vec[1:2, :] + vec[2:3, :], 0.0)
    b_out[...] = b_ref[...]
    invert(x_out, q_rows, slots, r_ref, q_ref, bh, bl)
    encode_ref(msg, MATRIX, x_out)


def first_side(x, one, two, three, four, f_out, msg, t_ref):
    unpack((one, two, three, four), SIDE, f_out)
    t_ref[...] = dot3(split(x[...]), split(f_out[...]))
    encode_ref(msg, SIDE, t_ref)


def second_matrix(b, low, high, vec, b_out, x_out, up, down, q_rows, slots, r_ref, q_ref, bh, bl):
    b_ref = slots.at[0]
    n = b.shape[0]
    eye = eye_mask(n)
    left, right = vec[1:2, :], vec[2:3, :]
    left_col, right_col = to_column(left, eye), to_column(right, eye)
    unpack((low,), MATRIX, b_ref)
    b_out[...] = b[...] - (left_col * b_ref[...]) * left
    unpack((high,), MATRIX, b_ref)
    b_out[...] -= (right_col * b_ref[...]) * right
    b_ref[...] = b_out[...]
    invert(x_out, q_rows, slots, r_ref, q_ref, bh, bl)
    b_ref[...] = (right_col * x_out[...]) * right
    encode_ref(up, MATRIX, b_ref)
    b_ref[...] = (left_col * x_out[...]) * left
    encode_ref(down, MATRIX, b_ref)


def second_side(x, f, low, high, vec, f_out, up, down, t_ref):
    eye = eye_mask(f.shape[0])
    left_col, right_col = to_column(vec[1:2, :], eye), to_column(vec[2:3, :], eye)
    unpack((low,), SIDE, t_ref)
    f_out[...] = f[...] + left_col * t_ref[...]
    unpack((high,), SIDE, t_ref)
    f_out[...] += right_col * t_ref[...]
    value = dot3(split(x[...]), split(f_out[...]))
    t_ref[...] = right_col * value
    encode_ref(up, SIDE, t_ref)
    t_ref[...] = left_col * value
    encode_ref(down, SIDE, t_ref)


def third_matrix(b, low, high, far_low, far_high, vec, x_out, g_ref, h_ref, q_rows, slots, r_ref, q_ref, bh, bl):
    b_ref = slots.at[0]
    n = b.shape[0]
    eye = eye_mask(n)
    b_ref[...] = b[...]
    for near, far, link in ((low, far_low, vec[1:2, :]), (high, far_high, vec[2:3, :])):
        unpack((near,), MATRIX, g_ref)
        unpack((far,), MATRIX, h_ref)
        g = split(g_ref[...])
        half = dot3(g, split(h_ref[...]))
        b_ref[...] -= (to_column(link, eye) * dot3(split(half), g)) * link
    invert(x_out, q_rows, slots, r_ref, q_ref, bh, bl)


def third_side(x, f, low, high, far_low, far_high, vec, msg, out16, g_ref, t_ref, s_ref):
    eye = eye_mask(f.shape[0])
    s_ref[...] = f[...]
    for near, far, link in ((low, far_low, vec[1:2, :]), (high, far_high, vec[2:3, :])):
        unpack((near,), MATRIX, g_ref)
        unpack((far,), SIDE, t_ref)
        s_ref[...] += to_column(link, eye) * dot3(split(g_ref[...]), split(t_ref[...]))
    t_ref[...] = dot3(split(x[...]), split(s_ref[...]))
    encode_ref(msg, SIDE, t_ref)
    out16[...] = t_ref[...].astype(BF16)


def predict(place, column, design, partial, code, two, three, out, residual, x_ref):
    n = out.shape[0]

    @pl.when(pl.program_id(0) == 0)
    def _():
        unpack((code,), SIDE, out)
        x_ref[0:n, :] = out[...].astype(BF16)
        x_ref[n : 2 * n, :] = two[...]
        x_ref[2 * n : 3 * n, :] = three[...]

    d = design[...]
    picked = []
    for m in (0, 2, 3):
        pick = jnp.where(column[...] == (place[0] ^ m), 1.0, 0.0)
        pick = jnp.broadcast_to(pick, (d.shape[0], STEP)).astype(BF16)
        picked.append(d * jnp.concatenate([pick] * (n // STEP), axis=1))
    residual[...] = partial[...] - dot1(jnp.concatenate(picked, axis=1), x_ref[...])


def call(kernel, outs, scratch, *args):
    return pl.pallas_call(kernel, out_shape=outs, scratch_shapes=scratch)(*args)


def gram(kernel, kept, msgs, place, *args):
    space = pl.BlockSpec(memory_space=pltpu.VMEM)
    specs = [pl.BlockSpec(memory_space=pltpu.SMEM)] + [space] * len(args)
    return pl.pallas_call(
        kernel,
        out_shape=kept + msgs,
        in_specs=specs,
        out_specs=(space,) * len(kept) + (pl.BlockSpec(memory_space=pl.ANY),) * len(msgs),
        scratch_shapes=[
            pltpu.VMEM((len(msgs),) + msgs[0].shape, jnp.int16),
            pltpu.SemaphoreType.DMA((len(msgs),)),
        ],
    )(place, *args)


def step_of(design, observed, row_interval, prior_ridge, coupling):
    row_count, n = design.shape
    count = lax.axis_size(PAIR)
    chain, place = lax.axis_index("chain"), lax.axis_index("arc")
    line = chain // 2
    time = LINE * line + 2 * jnp.where(line % 2 == 0, place, SLOTS - 1 - place) + chain % 2
    square = jax.ShapeDtypeStruct((n, n), F32)
    half = jax.ShapeDtypeStruct((n, n), BF16)
    matrix_msg = jax.ShapeDtypeStruct(MATRIX_MSG, jnp.int16)
    side_msg = jax.ShapeDtypeStruct(SIDE_MSG, jnp.int16)
    flat = row_interval.reshape(1, row_count)
    where = place.astype(jnp.int32).reshape(1)
    plain = [pltpu.VMEM((n, n), F32)]
    work = scratch_of(n)

    turned, *first = gram(
        functools.partial(gram_first, 3),
        (jax.ShapeDtypeStruct((n, row_count), BF16),),
        (matrix_msg,) * 2,
        where,
        flat,
        design,
    )
    rest = gram(functools.partial(gram_matrix, 1), (), (matrix_msg,) * 2, where, flat, turned, design)
    parts = first + list(rest)
    for i, m in enumerate(ROUNDS):
        parts[i] = to_seat(parts[i], m)
    side_parts = []
    for i in (0, 2):
        rounds = ROUNDS[i : i + 2]
        msgs = gram(functools.partial(gram_side, 3 - i), (), (side_msg,) * 2, where, flat, turned, observed)
        for j, m in enumerate(rounds):
            side_parts.append(to_seat(msgs[j], m))
    mine = carry(jnp.concatenate([prior_ridge, coupling], axis=0), home, seat)
    left_link = carry(coupling, home, lambda t: seat(t + 1) if t + 1 < count else None)
    right_link = jnp.where(time == count - 1, 0.0, mine[1:2])
    vec = jnp.concatenate([mine[0:1], left_link, right_link, jnp.zeros((5, n), F32)], axis=0)
    block, inverse, near = call(first_matrix, (square, square, matrix_msg), work, *parts, vec)
    low, high = along(near, 1), along(near, -1)
    side, near_side = call(first_side, (square, side_msg), plain, inverse, *side_parts)
    low_side, high_side = along(near_side, 1), along(near_side, -1)
    block_one, inverse_one, up, down = call(
        second_matrix, (square, square, matrix_msg, matrix_msg), work, block, low, high, vec
    )
    far_low, far_high = along(up, 2), along(down, -2)
    side_one, up_side, down_side = call(
        second_side, (square, side_msg, side_msg), plain, inverse_one, side, low_side, high_side, vec
    )
    far_low_side, far_high_side = along(up_side, 2), along(down_side, -2)
    inverse_two = call(third_matrix, square, plain * 2 + work, block_one, low, high, far_low, far_high, vec)
    code, rounded = call(
        third_side, (side_msg, half), plain * 3, inverse_two, side_one, low, high, far_low_side, far_high_side, vec
    )
    states = []
    for m in range(SLOTS):
        states.append(to_arc(rounded if m else code, m))
    picked = jnp.where((row_interval == (place ^ 1))[:, None], design, jnp.zeros((), design.dtype))
    partial = observed.astype(F32) - jnp.dot(picked, states[1], preferred_element_type=F32)
    chunk = row_count // SLOTS
    whole = pl.BlockSpec(memory_space=pltpu.VMEM)
    rows = lambda width: pl.BlockSpec((chunk, width), lambda i: (i, 0))
    solution, residual = pl.pallas_call(
        predict,
        grid=(SLOTS,),
        out_shape=(square, jax.ShapeDtypeStruct((row_count, n), F32)),
        in_specs=[pl.BlockSpec(memory_space=pltpu.SMEM), rows(1), rows(n), rows(n), whole, whole, whole],
        out_specs=(pl.BlockSpec((n, n), lambda i: (0, 0)), rows(n)),
        scratch_shapes=[pltpu.VMEM((3 * n, n), BF16)],
    )(where, row_interval.reshape(row_count, 1), design, partial, states[0], states[2], states[3])
    return (solution[None], residual)


def solution(mesh):
    placed = (P(PAIR, None), P(PAIR, None), P(PAIR), P(PAIR, None), P(PAIR, None))
    return jax.shard_map(
        step_of,
        mesh=mesh,
        in_specs=placed,
        out_specs=(P(PAIR, None, None), P(PAIR, None)),
        check_vma=False,
    )
```

```python
import functools

import jax
import jax.numpy as jnp
from jax import lax
from jax.experimental import pallas as pl
from jax.experimental.pallas import tpu as pltpu
from jax.sharding import PartitionSpec as P

F32 = jnp.float32
BF16 = jnp.bfloat16
PAIR = ("chain", "arc")


SLOTS = 4
LINE = 2 * SLOTS


def seat(t):
    line, spot = t // LINE, t % LINE
    chip = spot // 2 if line % 2 == 0 else SLOTS - 1 - spot // 2
    return (2 * line + spot % 2) * SLOTS + chip


def carry(value, source_of, target_of):
    count = lax.axis_size(PAIR)
    pairs = [(source_of(t), target_of(t)) for t in range(count)]
    return lax.ppermute(value, PAIR, [pair for pair in pairs if pair[1] is not None])


def along(value, steps):
    count = lax.axis_size(PAIR)
    return carry(value, seat, lambda t: seat(t + steps) if 0 <= t + steps < count else None)


def home(t):
    return t


def to_seat(value, m):
    return carry(value, lambda t: t - t % SLOTS + (t % SLOTS ^ m), seat)


def to_arc(value, m):
    return carry(value, seat, lambda t: t - t % SLOTS + (t % SLOTS ^ m))


def dot1(a, b):
    return lax.dot_general(a, b, (((1,), (0,)), ((), ())), preferred_element_type=F32)


def split(x):
    high = x.astype(BF16)
    return high, (x - high.astype(F32)).astype(BF16)


def dot3(a, b):
    (ah, al), (bh, bl) = a, b
    return dot1(ah, bh) + (dot1(ah, bl) + dot1(al, bh))


def dot_full(a, b):
    return lax.dot_general(
        a, b, (((1,), (0,)), ((), ())), precision=lax.Precision.HIGHEST, preferred_element_type=F32
    )


def eye_mask(n):
    return lax.broadcasted_iota(jnp.int32, (n, n), 0) == lax.broadcasted_iota(jnp.int32, (n, n), 1)


def to_column(row, eye):
    return jnp.sum(jnp.where(eye, row, 0.0), axis=1, keepdims=True)


def invert(x_ref, q_rows, slots, r_ref, q_ref, bh_ref, bl_ref):
    n = x_ref.shape[0]
    b_ref = slots.at[0]
    eye = eye_mask(n)
    one = jnp.where(eye, 1.0, 0.0).astype(F32)
    b = b_ref[...]
    picked = jnp.where(eye, b, 0.0)
    s_row = lax.rsqrt(jnp.sum(picked, axis=0, keepdims=True))
    s_col = lax.rsqrt(jnp.sum(picked, axis=1, keepdims=True))
    b = b * s_row * s_col
    b_ref[...] = b
    high, low = split(b)
    bh_ref[...] = high
    bl_ref[...] = low
    x_ref[...] = one - b
    r0 = x_ref[...].astype(BF16)
    square = dot1(r0, r0)
    r_ref[...] = square.astype(BF16)
    fourth = dot1(r_ref[...], r_ref[...])
    well = jnp.sum(fourth * fourth) < 0.9
    q_ref[...] = fourth.astype(BF16)

    @pl.when(well)
    def _():
        x_ref[...] += jnp.where(eye_mask(n), 1.0, 0.0)
        x_ref[...] += dot1(x_ref[...].astype(BF16), r_ref[...])
        x_ref[...] += dot1(x_ref[...].astype(BF16), q_ref[...])

        def step(carry):
            count, _ = carry
            residual = jnp.where(eye_mask(n), 1.0, 0.0) - dot3(
                (bh_ref[...], bl_ref[...]), split(x_ref[...])
            )
            r_ref[...] = residual.astype(BF16)
            x_ref[...] += dot1(x_ref[...].astype(BF16), r_ref[...])
            return count + 1, jnp.sum(residual * residual)

        lax.while_loop(
            lambda carry: jnp.logical_and(carry[0] < 12, carry[1] > 4e-5),
            step,
            (jnp.int32(0), jnp.float32(1.0)),
        )

    @pl.when(jnp.logical_not(well))
    def _():
        def rows_of(i, size=PART):
            return pl.ds(pl.multiple_of(i * size, size), size)

        def ones_of(i):
            spot = lax.broadcasted_iota(jnp.int32, (PART, n), 0) + i * PART
            return jnp.where(spot == lax.broadcasted_iota(jnp.int32, (PART, n), 1), 1.0, 0.0)

        def widest(i, largest):
            return jnp.maximum(largest, jnp.max(jnp.sum(jnp.abs(slots[0, rows_of(i), :]), axis=1, keepdims=True)))

        alpha = 2.0 / (1.0 + lax.fori_loop(0, n // PART, widest, jnp.float32(1.0)))

        def start(i, _):
            slots[1, rows_of(i), :] = alpha * ones_of(i)
            return 0

        lax.fori_loop(0, n // PART, start, 0)

        def phase(number, total):
            first, second = number // (n // PART), number % (n // PART)
            row = rows_of(second)
            pl.when(first == 0)(lambda: slots.__setitem__((2, row, slice(None)), ones_of(second)))
            q_rows[...] = slots[first, row, :]
            sign = (2 * first - 1).astype(F32)

            def add(number, _):
                k, j = rows_of(number // (n // STEP), STEP), rows_of(number % (n // STEP), STEP)
                slots[2 - first, row, j] += sign * dot_full(q_rows[:, k], slots[1 + first, k, j])
                return 0

            lax.fori_loop(0, (n // STEP) ** 2, add, 0)
            return total + jnp.where(first == 0, jnp.sum(slots[2, row, :] * slots[2, row, :]), 0.0)

        lax.while_loop(
            lambda carry: jnp.logical_and(carry[0] < 60, carry[1] > 1e-7),
            lambda carry: (carry[0] + 1, lax.fori_loop(0, 2 * (n // PART), phase, jnp.float32(0.0))),
            (jnp.int32(0), jnp.float32(1.0)),
        )

        def finish(i, _):
            x_ref[rows_of(i), :] = slots[1, rows_of(i), :]
            return 0

        lax.fori_loop(0, n // PART, finish, 0)

    x_ref[...] = x_ref[...] * s_row * s_col


STEP = 128
PART = 32
GRAIN = 1.0 / 128.0
FULL = 32767.0
FINE = 4194304.0
SHIFT = 13000.0
MATRIX = ((0, 80, ((384, 4), (0, 1))), (5, 81, ((256, 3), (128, 2))))
SIDE = ((0, 128, ((0, 4), (128, 4), (256, 4), (384, 4))),)
MATRIX_MSG = (82, 16, 128)
SIDE_MSG = (129, 16, 128)


def power_of(size):
    return jnp.ceil(jnp.log2(jnp.maximum(size, 1e-30)) * STEP)


def to_tiles(value):
    return jnp.clip(jnp.round(value), -FULL, FULL).astype(jnp.int32).astype(jnp.int16)


def encode(msg, plan, piece_of):
    lane = lax.broadcasted_iota(jnp.int32, (STEP, STEP), 1)
    eye = eye_mask(STEP)
    for first, spot, pieces in plan:
        scales = jnp.zeros((STEP, STEP), F32)
        place = 8 * first
        for number, (row, wide) in enumerate(pieces):
            piece = piece_of(row, wide * STEP)
            blocks = [piece[:, i * STEP : i * STEP + STEP] for i in range(wide)]
            if plan is MATRIX:
                own = jnp.sum(jnp.where(eye, blocks[-1], 0.0), axis=1, keepdims=True)
                blocks[-1] = jnp.where(eye, 0.0, blocks[-1])
                power = power_of(jnp.abs(own))
                fine = (own * jnp.exp2(power * (-GRAIN)) - 1.0) * FINE
                scales = jnp.where(lane == 4 + number, power + SHIFT, scales)
                scales = jnp.where(lane == 6 + number, fine, scales)
            size = functools.reduce(jnp.maximum, [jnp.abs(block) for block in blocks])
            power = power_of(jnp.max(size, axis=1, keepdims=True))
            unit = jnp.exp2(power * (-GRAIN)) * FULL
            scales = jnp.where(lane == number, power + SHIFT, scales)
            for block in blocks:
                msg[place : place + 8] = to_tiles(block * unit).reshape(8, 16, STEP)
                place += 8
        msg[spot] = to_tiles(scales.T[0:16, :])


def encode_ref(msg, plan, ref):
    encode(msg, plan, lambda row, width: ref[row : row + STEP, 0:width])


def decode(msg, plan):
    eye = eye_mask(STEP)
    for first, spot, pieces in plan:
        flat = msg[spot].astype(jnp.int32).astype(F32)
        codes = jnp.concatenate([flat, jnp.zeros((STEP - 16, STEP), F32)], axis=0).T
        powers = jnp.exp2((codes - SHIFT) * GRAIN)
        place = 8 * first
        for number, (row, wide) in enumerate(pieces):
            unit = powers[:, number : number + 1] * (1.0 / FULL)
            blocks = []
            for _ in range(wide):
                blocks.append(msg[place : place + 8].reshape(STEP, STEP).astype(jnp.int32).astype(F32) * unit)
                place += 8
            if plan is MATRIX:
                own = powers[:, 4 + number : 5 + number] * (1.0 + codes[:, 6 + number : 7 + number] * (1.0 / FINE))
                blocks[-1] = jnp.where(eye, own, blocks[-1])
            yield row, wide * STEP, jnp.concatenate(blocks, axis=1)


def unpack(msgs, plan, target):
    for pieces in zip(*(decode(msg, plan) for msg in msgs)):
        row, width, _ = pieces[0]
        target[row : row + STEP, 0:width] = functools.reduce(lambda p, q: p + q, [piece[2] for piece in pieces])
    if plan is MATRIX:
        for i in range(4):
            for j in range(i):
                target[j * STEP : j * STEP + STEP, i * STEP : i * STEP + STEP] = target[
                    i * STEP : i * STEP + STEP, j * STEP : j * STEP + STEP
                ].T


def scratch_of(n):
    return [
        pltpu.VMEM((PART, n), F32),
        pltpu.VMEM((3, n, n), F32),
        pltpu.VMEM((n, n), BF16),
        pltpu.VMEM((n, n), BF16),
        pltpu.VMEM((n, n), BF16),
        pltpu.VMEM((n, n), BF16),
    ]


def masked(slot, row_interval, turned):
    pick = jnp.where(row_interval[...] == slot, 1.0, 0.0).astype(BF16)
    return turned[...] * pick


ROUNDS = (3, 2, 1, 0)


def each_round(base, place, row_interval, turned, plan, other, msgs, buf, sems):
    def out(i):
        return pltpu.make_async_copy(buf.at[i], msgs[i], sems.at[i])

    def one(i, _):
        left = masked(place[0] ^ (base - i), row_interval, turned)
        encode(buf.at[i], plan, lambda row, width: dot1(left[row : row + STEP, :], other[:, 0:width]))
        for j in range(len(msgs)):
            pl.when(i == j)(lambda: out(j).start())
        return 0

    lax.fori_loop(0, len(msgs), one, 0)
    for j in range(len(msgs)):
        out(j).wait()


def gram_matrix(place, row_interval, design, turned, *msgs):
    turned[...] = design[...].T
    for m, msg in zip(ROUNDS, msgs):
        left = masked(place[0] ^ m, row_interval, turned)
        encode(msg, MATRIX, lambda row, width: dot1(left[row : row + STEP, :], design[:, 0:width]))


def gram_side(base, place, row_interval, turned, observed, *rest):
    each_round(base, place, row_interval, turned, SIDE, observed, rest[:-2], *rest[-2:])


def first_matrix(one, two, three, four, vec, b_out, x_out, msg, q_rows, slots, r_ref, q_ref, bh, bl):
    b_ref = slots.at[0]
    n = b_out.shape[0]
    unpack((one, two, three, four), MATRIX, b_ref)
    b_ref[...] += jnp.where(eye_mask(n), vec[0:1, :] + vec[1:2, :] + vec[2:3, :], 0.0)
    b_out[...] = b_ref[...]
    invert(x_out, q_rows, slots, r_ref, q_ref, bh, bl)
    encode_ref(msg, MATRIX, x_out)


def first_side(x, one, two, three, four, f_out, msg, t_ref):
    unpack((one, two, three, four), SIDE, f_out)
    t_ref[...] = dot3(split(x[...]), split(f_out[...]))
    encode_ref(msg, SIDE, t_ref)


def second_matrix(b, low, high, vec, b_out, x_out, up, down, q_rows, slots, r_ref, q_ref, bh, bl):
    b_ref = slots.at[0]
    n = b.shape[0]
    eye = eye_mask(n)
    left, right = vec[1:2, :], vec[2:3, :]
    left_col, right_col = to_column(left, eye), to_column(right, eye)
    unpack((low,), MATRIX, b_ref)
    b_out[...] = b[...] - (left_col * b_ref[...]) * left
    unpack((high,), MATRIX, b_ref)
    b_out[...] -= (right_col * b_ref[...]) * right
    b_ref[...] = b_out[...]
    invert(x_out, q_rows, slots, r_ref, q_ref, bh, bl)
    b_ref[...] = (right_col * x_out[...]) * right
    encode_ref(up, MATRIX, b_ref)
    b_ref[...] = (left_col * x_out[...]) * left
    encode_ref(down, MATRIX, b_ref)


def second_side(x, f, low, high, vec, f_out, up, down, t_ref):
    eye = eye_mask(f.shape[0])
    left_col, right_col = to_column(vec[1:2, :], eye), to_column(vec[2:3, :], eye)
    unpack((low,), SIDE, t_ref)
    f_out[...] = f[...] + left_col * t_ref[...]
    unpack((high,), SIDE, t_ref)
    f_out[...] += right_col * t_ref[...]
    value = dot3(split(x[...]), split(f_out[...]))
    t_ref[...] = right_col * value
    encode_ref(up, SIDE, t_ref)
    t_ref[...] = left_col * value
    encode_ref(down, SIDE, t_ref)


def third_matrix(b, low, high, far_low, far_high, vec, x_out, g_ref, h_ref, q_rows, slots, r_ref, q_ref, bh, bl):
    b_ref = slots.at[0]
    n = b.shape[0]
    eye = eye_mask(n)
    b_ref[...] = b[...]
    for near, far, link in ((low, far_low, vec[1:2, :]), (high, far_high, vec[2:3, :])):
        unpack((near,), MATRIX, g_ref)
        unpack((far,), MATRIX, h_ref)
        g = split(g_ref[...])
        half = dot3(g, split(h_ref[...]))
        b_ref[...] -= (to_column(link, eye) * dot3(split(half), g)) * link
    invert(x_out, q_rows, slots, r_ref, q_ref, bh, bl)


def third_side(x, f, low, high, far_low, far_high, vec, msg, out16, g_ref, t_ref, s_ref):
    eye = eye_mask(f.shape[0])
    s_ref[...] = f[...]
    for near, far, link in ((low, far_low, vec[1:2, :]), (high, far_high, vec[2:3, :])):
        unpack((near,), MATRIX, g_ref)
        unpack((far,), SIDE, t_ref)
        s_ref[...] += to_column(link, eye) * dot3(split(g_ref[...]), split(t_ref[...]))
    t_ref[...] = dot3(split(x[...]), split(s_ref[...]))
    encode_ref(msg, SIDE, t_ref)
    out16[...] = t_ref[...].astype(BF16)


def predict(place, column, design, observed, code, one, two, three, out, residual, x_ref):
    n = out.shape[0]

    @pl.when(pl.program_id(0) == 0)
    def _():
        unpack((code,), SIDE, out)
        x_ref[0:n, :] = out[...].astype(BF16)
        x_ref[n : 2 * n, :] = one[...]
        x_ref[2 * n : 3 * n, :] = two[...]
        x_ref[3 * n : 4 * n, :] = three[...]

    d = design[...]
    picked = []
    for m in range(SLOTS):
        pick = jnp.where(column[...] == (place[0] ^ m), 1.0, 0.0)
        pick = jnp.broadcast_to(pick, (d.shape[0], STEP)).astype(BF16)
        picked.append(d * jnp.concatenate([pick] * (n // STEP), axis=1))
    residual[...] = observed[...].astype(F32) - dot1(jnp.concatenate(picked, axis=1), x_ref[...])


def call(kernel, outs, scratch, *args):
    return pl.pallas_call(kernel, out_shape=outs, scratch_shapes=scratch)(*args)


def gram(kernel, msgs, place, *args):
    space = pl.BlockSpec(memory_space=pltpu.VMEM)
    specs = [pl.BlockSpec(memory_space=pltpu.SMEM)] + [space] * len(args)
    return pl.pallas_call(
        kernel,
        out_shape=msgs,
        in_specs=specs,
        out_specs=(pl.BlockSpec(memory_space=pl.ANY),) * len(msgs),
        scratch_shapes=[
            pltpu.VMEM((len(msgs),) + msgs[0].shape, jnp.int16),
            pltpu.SemaphoreType.DMA((len(msgs),)),
        ],
    )(place, *args)


def step_of(design, observed, row_interval, prior_ridge, coupling):
    row_count, n = design.shape
    count = lax.axis_size(PAIR)
    chain, place = lax.axis_index("chain"), lax.axis_index("arc")
    line = chain // 2
    time = LINE * line + 2 * jnp.where(line % 2 == 0, place, SLOTS - 1 - place) + chain % 2
    square = jax.ShapeDtypeStruct((n, n), F32)
    half = jax.ShapeDtypeStruct((n, n), BF16)
    matrix_msg = jax.ShapeDtypeStruct(MATRIX_MSG, jnp.int16)
    side_msg = jax.ShapeDtypeStruct(SIDE_MSG, jnp.int16)
    flat = row_interval.reshape(1, row_count)
    where = place.astype(jnp.int32).reshape(1)
    plain = [pltpu.VMEM((n, n), F32)]
    work = scratch_of(n)

    space = pl.BlockSpec(memory_space=pltpu.VMEM)
    turned, *parts = pl.pallas_call(
        gram_matrix,
        out_shape=(jax.ShapeDtypeStruct((n, row_count), BF16),) + (matrix_msg,) * SLOTS,
        in_specs=[pl.BlockSpec(memory_space=pltpu.SMEM), space, space],
    )(where, flat, design)
    for i, m in enumerate(ROUNDS):
        parts[i] = to_seat(parts[i], m)
    side_parts = []
    for i in (0, 2):
        rounds = ROUNDS[i : i + 2]
        msgs = gram(functools.partial(gram_side, 3 - i), (side_msg,) * 2, where, flat, turned, observed)
        for j, m in enumerate(rounds):
            side_parts.append(to_seat(msgs[j], m))
    mine = carry(jnp.concatenate([prior_ridge, coupling], axis=0), home, seat)
    left_link = carry(coupling, home, lambda t: seat(t + 1) if t + 1 < count else None)
    right_link = jnp.where(time == count - 1, 0.0, mine[1:2])
    vec = jnp.concatenate([mine[0:1], left_link, right_link, jnp.zeros((5, n), F32)], axis=0)
    block, inverse, near = call(first_matrix, (square, square, matrix_msg), work, *parts, vec)
    low, high = along(near, 1), along(near, -1)
    side, near_side = call(first_side, (square, side_msg), plain, inverse, *side_parts)
    low_side, high_side = along(near_side, 1), along(near_side, -1)
    block_one, inverse_one, up, down = call(
        second_matrix, (square, square, matrix_msg, matrix_msg), work, block, low, high, vec
    )
    far_low, far_high = along(up, 2), along(down, -2)
    side_one, up_side, down_side = call(
        second_side, (square, side_msg, side_msg), plain, inverse_one, side, low_side, high_side, vec
    )
    far_low_side, far_high_side = along(up_side, 2), along(down_side, -2)
    inverse_two = call(third_matrix, square, plain * 2 + work, block_one, low, high, far_low, far_high, vec)
    code, rounded = call(
        third_side, (side_msg, half), plain * 3, inverse_two, side_one, low, high, far_low_side, far_high_side, vec
    )
    states = []
    for m in range(SLOTS):
        states.append(to_arc(rounded if m else code, m))
    chunk = row_count // SLOTS
    whole = pl.BlockSpec(memory_space=pltpu.VMEM)
    rows = lambda width: pl.BlockSpec((chunk, width), lambda i: (i, 0))
    solution, residual = pl.pallas_call(
        predict,
        grid=(SLOTS,),
        out_shape=(square, jax.ShapeDtypeStruct((row_count, n), F32)),
        in_specs=[pl.BlockSpec(memory_space=pltpu.SMEM), rows(1), rows(n), rows(n)] + [whole] * SLOTS,
        out_specs=(pl.BlockSpec((n, n), lambda i: (0, 0)), rows(n)),
        scratch_shapes=[pltpu.VMEM((SLOTS * n, n), BF16)],
    )(where, row_interval.reshape(row_count, 1), design, observed, *states)
    return (solution[None], residual)


def solution(mesh):
    placed = (P(PAIR, None), P(PAIR, None), P(PAIR), P(PAIR, None), P(PAIR, None))
    return jax.shard_map(
        step_of,
        mesh=mesh,
        in_specs=placed,
        out_specs=(P(PAIR, None, None), P(PAIR, None)),
        check_vma=False,
    )
```

```python
import functools

import jax
import jax.numpy as jnp
from jax import lax
from jax.experimental import pallas as pl
from jax.experimental.pallas import tpu as pltpu
from jax.sharding import PartitionSpec as P

F32 = jnp.float32
BF16 = jnp.bfloat16
PAIR = ("chain", "arc")


SLOTS = 4
LINE = 2 * SLOTS


def seat(t):
    line, spot = t // LINE, t % LINE
    chip = spot // 2 if line % 2 == 0 else SLOTS - 1 - spot // 2
    return (2 * line + spot % 2) * SLOTS + chip


def carry(value, source_of, target_of):
    count = lax.axis_size(PAIR)
    pairs = [(source_of(t), target_of(t)) for t in range(count)]
    return lax.ppermute(value, PAIR, [pair for pair in pairs if pair[1] is not None])


def along(value, steps):
    count = lax.axis_size(PAIR)
    return carry(value, seat, lambda t: seat(t + steps) if 0 <= t + steps < count else None)


def home(t):
    return t


def to_seat(value, m):
    return carry(value, lambda t: t - t % SLOTS + (t % SLOTS ^ m), seat)


def to_arc(value, m):
    return carry(value, seat, lambda t: t - t % SLOTS + (t % SLOTS ^ m))


def dot1(a, b):
    return lax.dot_general(a, b, (((1,), (0,)), ((), ())), preferred_element_type=F32)


def split(x):
    high = x.astype(BF16)
    return high, (x - high.astype(F32)).astype(BF16)


def dot3(a, b):
    (ah, al), (bh, bl) = a, b
    return dot1(ah, bh) + (dot1(ah, bl) + dot1(al, bh))


def dot_full(a, b):
    return lax.dot_general(
        a, b, (((1,), (0,)), ((), ())), precision=lax.Precision.HIGHEST, preferred_element_type=F32
    )


def eye_mask(n):
    return lax.broadcasted_iota(jnp.int32, (n, n), 0) == lax.broadcasted_iota(jnp.int32, (n, n), 1)


def to_column(row, eye):
    return jnp.sum(jnp.where(eye, row, 0.0), axis=1, keepdims=True)


def invert(x_ref, q_rows, slots, r_ref, q_ref, bh_ref, bl_ref):
    n = x_ref.shape[0]
    b_ref = slots.at[0]
    eye = eye_mask(n)
    one = jnp.where(eye, 1.0, 0.0).astype(F32)
    b = b_ref[...]
    picked = jnp.where(eye, b, 0.0)
    s_row = lax.rsqrt(jnp.sum(picked, axis=0, keepdims=True))
    s_col = lax.rsqrt(jnp.sum(picked, axis=1, keepdims=True))
    b = b * s_row * s_col
    b_ref[...] = b
    high, low = split(b)
    bh_ref[...] = high
    bl_ref[...] = low
    x_ref[...] = one - b
    r0 = x_ref[...].astype(BF16)
    square = dot1(r0, r0)
    r_ref[...] = square.astype(BF16)
    fourth = dot1(r_ref[...], r_ref[...])
    well = jnp.sum(fourth * fourth) < 0.9
    q_ref[...] = fourth.astype(BF16)

    @pl.when(well)
    def _():
        x_ref[...] += jnp.where(eye_mask(n), 1.0, 0.0)
        x_ref[...] += dot1(x_ref[...].astype(BF16), r_ref[...])
        x_ref[...] += dot1(x_ref[...].astype(BF16), q_ref[...])

        def step(carry):
            count, _ = carry
            residual = jnp.where(eye_mask(n), 1.0, 0.0) - dot3(
                (bh_ref[...], bl_ref[...]), split(x_ref[...])
            )
            r_ref[...] = residual.astype(BF16)
            x_ref[...] += dot1(x_ref[...].astype(BF16), r_ref[...])
            return count + 1, jnp.sum(residual * residual)

        lax.while_loop(
            lambda carry: jnp.logical_and(carry[0] < 12, carry[1] > 4e-5),
            step,
            (jnp.int32(0), jnp.float32(1.0)),
        )

    @pl.when(jnp.logical_not(well))
    def _():
        def rows_of(i, size=PART):
            return pl.ds(pl.multiple_of(i * size, size), size)

        def ones_of(i):
            spot = lax.broadcasted_iota(jnp.int32, (PART, n), 0) + i * PART
            return jnp.where(spot == lax.broadcasted_iota(jnp.int32, (PART, n), 1), 1.0, 0.0)

        def widest(i, largest):
            return jnp.maximum(largest, jnp.max(jnp.sum(jnp.abs(slots[0, rows_of(i), :]), axis=1, keepdims=True)))

        alpha = 2.0 / (1.0 + lax.fori_loop(0, n // PART, widest, jnp.float32(1.0)))

        def start(i, _):
            slots[1, rows_of(i), :] = alpha * ones_of(i)
            return 0

        lax.fori_loop(0, n // PART, start, 0)

        def phase(number, total):
            first, second = number // (n // PART), number % (n // PART)
            row = rows_of(second)
            pl.when(first == 0)(lambda: slots.__setitem__((2, row, slice(None)), ones_of(second)))
            q_rows[...] = slots[first, row, :]
            sign = (2 * first - 1).astype(F32)

            def add(number, _):
                k, j = rows_of(number // (n // STEP), STEP), rows_of(number % (n // STEP), STEP)
                slots[2 - first, row, j] += sign * dot_full(q_rows[:, k], slots[1 + first, k, j])
                return 0

            lax.fori_loop(0, (n // STEP) ** 2, add, 0)
            return total + jnp.where(first == 0, jnp.sum(slots[2, row, :] * slots[2, row, :]), 0.0)

        lax.while_loop(
            lambda carry: jnp.logical_and(carry[0] < 60, carry[1] > 1e-7),
            lambda carry: (carry[0] + 1, lax.fori_loop(0, 2 * (n // PART), phase, jnp.float32(0.0))),
            (jnp.int32(0), jnp.float32(1.0)),
        )

        def finish(i, _):
            x_ref[rows_of(i), :] = slots[1, rows_of(i), :]
            return 0

        lax.fori_loop(0, n // PART, finish, 0)

    x_ref[...] = x_ref[...] * s_row * s_col


STEP = 128
PART = 32
GRAIN = 1.0 / 128.0
FULL = 32767.0
FINE = 4194304.0
SHIFT = 13000.0
MATRIX = ((0, 80, ((384, 4), (0, 1))), (5, 81, ((256, 3), (128, 2))))
SIDE = ((0, 128, ((0, 4), (128, 4), (256, 4), (384, 4))),)
MATRIX_MSG = (82, 16, 128)
SIDE_MSG = (129, 16, 128)


def power_of(size):
    return jnp.ceil(jnp.log2(jnp.maximum(size, 1e-30)) * STEP)


def to_tiles(value):
    return jnp.clip(jnp.round(value), -FULL, FULL).astype(jnp.int32).astype(jnp.int16)


def encode(msg, plan, piece_of):
    lane = lax.broadcasted_iota(jnp.int32, (STEP, STEP), 1)
    eye = eye_mask(STEP)
    for first, spot, pieces in plan:
        scales = jnp.zeros((STEP, STEP), F32)
        place = 8 * first
        for number, (row, wide) in enumerate(pieces):
            piece = piece_of(row, wide * STEP)
            blocks = [piece[:, i * STEP : i * STEP + STEP] for i in range(wide)]
            if plan is MATRIX:
                own = jnp.sum(jnp.where(eye, blocks[-1], 0.0), axis=1, keepdims=True)
                blocks[-1] = jnp.where(eye, 0.0, blocks[-1])
                power = power_of(jnp.abs(own))
                fine = (own * jnp.exp2(power * (-GRAIN)) - 1.0) * FINE
                scales = jnp.where(lane == 4 + number, power + SHIFT, scales)
                scales = jnp.where(lane == 6 + number, fine, scales)
            size = functools.reduce(jnp.maximum, [jnp.abs(block) for block in blocks])
            power = power_of(jnp.max(size, axis=1, keepdims=True))
            unit = jnp.exp2(power * (-GRAIN)) * FULL
            scales = jnp.where(lane == number, power + SHIFT, scales)
            for block in blocks:
                msg[place : place + 8] = to_tiles(block * unit).reshape(8, 16, STEP)
                place += 8
        msg[spot] = to_tiles(scales.T[0:16, :])


def encode_ref(msg, plan, ref):
    encode(msg, plan, lambda row, width: ref[row : row + STEP, 0:width])


def decode(msg, plan):
    eye = eye_mask(STEP)
    for first, spot, pieces in plan:
        flat = msg[spot].astype(jnp.int32).astype(F32)
        codes = jnp.concatenate([flat, jnp.zeros((STEP - 16, STEP), F32)], axis=0).T
        powers = jnp.exp2((codes - SHIFT) * GRAIN)
        place = 8 * first
        for number, (row, wide) in enumerate(pieces):
            unit = powers[:, number : number + 1] * (1.0 / FULL)
            blocks = []
            for _ in range(wide):
                blocks.append(msg[place : place + 8].reshape(STEP, STEP).astype(jnp.int32).astype(F32) * unit)
                place += 8
            if plan is MATRIX:
                own = powers[:, 4 + number : 5 + number] * (1.0 + codes[:, 6 + number : 7 + number] * (1.0 / FINE))
                blocks[-1] = jnp.where(eye, own, blocks[-1])
            yield row, wide * STEP, jnp.concatenate(blocks, axis=1)


def unpack(msgs, plan, target):
    for pieces in zip(*(decode(msg, plan) for msg in msgs)):
        row, width, _ = pieces[0]
        target[row : row + STEP, 0:width] = functools.reduce(lambda p, q: p + q, [piece[2] for piece in pieces])
    if plan is MATRIX:
        for i in range(4):
            for j in range(i):
                target[j * STEP : j * STEP + STEP, i * STEP : i * STEP + STEP] = target[
                    i * STEP : i * STEP + STEP, j * STEP : j * STEP + STEP
                ].T


def scratch_of(n):
    return [
        pltpu.VMEM((PART, n), F32),
        pltpu.VMEM((3, n, n), F32),
        pltpu.VMEM((n, n), BF16),
        pltpu.VMEM((n, n), BF16),
        pltpu.VMEM((n, n), BF16),
        pltpu.VMEM((n, n), BF16),
    ]


def masked(slot, row_interval, turned):
    pick = jnp.where(row_interval[...] == slot, 1.0, 0.0).astype(BF16)
    return turned[...] * pick


ROUNDS = (3, 2, 1, 0)


def each_round(base, place, row_interval, turned, plan, other, msgs, buf, sems):
    def out(i):
        return pltpu.make_async_copy(buf.at[i], msgs[i], sems.at[i])

    def one(i, _):
        left = masked(place[0] ^ (base - i), row_interval, turned)
        encode(buf.at[i], plan, lambda row, width: dot1(left[row : row + STEP, :], other[:, 0:width]))
        for j in range(len(msgs)):
            pl.when(i == j)(lambda: out(j).start())
        return 0

    lax.fori_loop(0, len(msgs), one, 0)
    for j in range(len(msgs)):
        out(j).wait()


def gram_matrix(place, row_interval, design, turned, *msgs):
    turned[...] = design[...].T
    for m, msg in zip(ROUNDS, msgs):
        left = masked(place[0] ^ m, row_interval, turned)
        encode(msg, MATRIX, lambda row, width: dot1(left[row : row + STEP, :], design[:, 0:width]))


def gram_side(base, place, row_interval, turned, observed, *rest):
    each_round(base, place, row_interval, turned, SIDE, observed, rest[:-2], *rest[-2:])


def first_matrix(one, two, three, four, vec, b_out, x_out, msg, q_rows, slots, r_ref, q_ref, bh, bl):
    b_ref = slots.at[0]
    n = b_out.shape[0]
    unpack((one, two, three, four), MATRIX, b_ref)
    b_ref[...] += jnp.where(eye_mask(n), vec[0:1, :] + vec[1:2, :] + vec[2:3, :], 0.0)
    b_out[...] = b_ref[...]
    invert(x_out, q_rows, slots, r_ref, q_ref, bh, bl)
    encode_ref(msg, MATRIX, x_out)


def first_side(x, one, two, three, four, f_out, msg, t_ref):
    unpack((one, two, three, four), SIDE, f_out)
    t_ref[...] = dot3(split(x[...]), split(f_out[...]))
    encode_ref(msg, SIDE, t_ref)


def second_matrix(b, low, high, vec, b_out, x_out, up, down, q_rows, slots, r_ref, q_ref, bh, bl):
    b_ref = slots.at[0]
    n = b.shape[0]
    eye = eye_mask(n)
    left, right = vec[1:2, :], vec[2:3, :]
    left_col, right_col = to_column(left, eye), to_column(right, eye)
    unpack((low,), MATRIX, b_ref)
    b_out[...] = b[...] - (left_col * b_ref[...]) * left
    unpack((high,), MATRIX, b_ref)
    b_out[...] -= (right_col * b_ref[...]) * right
    b_ref[...] = b_out[...]
    invert(x_out, q_rows, slots, r_ref, q_ref, bh, bl)
    b_ref[...] = (right_col * x_out[...]) * right
    encode_ref(up, MATRIX, b_ref)
    b_ref[...] = (left_col * x_out[...]) * left
    encode_ref(down, MATRIX, b_ref)


def second_side(x, f, low, high, vec, f_out, up, down, t_ref):
    eye = eye_mask(f.shape[0])
    left_col, right_col = to_column(vec[1:2, :], eye), to_column(vec[2:3, :], eye)
    unpack((low,), SIDE, t_ref)
    f_out[...] = f[...] + left_col * t_ref[...]
    unpack((high,), SIDE, t_ref)
    f_out[...] += right_col * t_ref[...]
    value = dot3(split(x[...]), split(f_out[...]))
    t_ref[...] = right_col * value
    encode_ref(up, SIDE, t_ref)
    t_ref[...] = left_col * value
    encode_ref(down, SIDE, t_ref)


def third_matrix(b, low, high, far_low, far_high, vec, x_out, g_ref, h_ref, q_rows, slots, r_ref, q_ref, bh, bl):
    b_ref = slots.at[0]
    n = b.shape[0]
    eye = eye_mask(n)
    b_ref[...] = b[...]
    for near, far, link in ((low, far_low, vec[1:2, :]), (high, far_high, vec[2:3, :])):
        unpack((near,), MATRIX, g_ref)
        unpack((far,), MATRIX, h_ref)
        g = split(g_ref[...])
        half = dot3(g, split(h_ref[...]))
        b_ref[...] -= (to_column(link, eye) * dot3(split(half), g)) * link
    invert(x_out, q_rows, slots, r_ref, q_ref, bh, bl)


def third_side(x, f, low, high, far_low, far_high, vec, msg, out16, g_ref, t_ref, s_ref):
    eye = eye_mask(f.shape[0])
    s_ref[...] = f[...]
    for near, far, link in ((low, far_low, vec[1:2, :]), (high, far_high, vec[2:3, :])):
        unpack((near,), MATRIX, g_ref)
        unpack((far,), SIDE, t_ref)
        s_ref[...] += to_column(link, eye) * dot3(split(g_ref[...]), split(t_ref[...]))
    t_ref[...] = dot3(split(x[...]), split(s_ref[...]))
    encode_ref(msg, SIDE, t_ref)
    out16[...] = t_ref[...].astype(BF16)


def predict(place, column, design, partial, code, two, three, out, residual, x_ref):
    n = out.shape[0]

    @pl.when(pl.program_id(0) == 0)
    def _():
        unpack((code,), SIDE, out)
        x_ref[0:n, :] = out[...].astype(BF16)
        x_ref[n : 2 * n, :] = two[...]
        x_ref[2 * n : 3 * n, :] = three[...]

    d = design[...]
    picked = []
    for m in (0, 2, 3):
        pick = jnp.where(column[...] == (place[0] ^ m), 1.0, 0.0)
        pick = jnp.broadcast_to(pick, (d.shape[0], STEP)).astype(BF16)
        picked.append(d * jnp.concatenate([pick] * (n // STEP), axis=1))
    residual[...] = partial[...] - dot1(jnp.concatenate(picked, axis=1), x_ref[...])


def call(kernel, outs, scratch, *args):
    return pl.pallas_call(kernel, out_shape=outs, scratch_shapes=scratch)(*args)


def gram(kernel, msgs, place, *args):
    space = pl.BlockSpec(memory_space=pltpu.VMEM)
    specs = [pl.BlockSpec(memory_space=pltpu.SMEM)] + [space] * len(args)
    return pl.pallas_call(
        kernel,
        out_shape=msgs,
        in_specs=specs,
        out_specs=(pl.BlockSpec(memory_space=pl.ANY),) * len(msgs),
        scratch_shapes=[
            pltpu.VMEM((len(msgs),) + msgs[0].shape, jnp.int16),
            pltpu.SemaphoreType.DMA((len(msgs),)),
        ],
    )(place, *args)


def step_of(design, observed, row_interval, prior_ridge, coupling):
    row_count, n = design.shape
    count = lax.axis_size(PAIR)
    chain, place = lax.axis_index("chain"), lax.axis_index("arc")
    line = chain // 2
    time = LINE * line + 2 * jnp.where(line % 2 == 0, place, SLOTS - 1 - place) + chain % 2
    square = jax.ShapeDtypeStruct((n, n), F32)
    half = jax.ShapeDtypeStruct((n, n), BF16)
    matrix_msg = jax.ShapeDtypeStruct(MATRIX_MSG, jnp.int16)
    side_msg = jax.ShapeDtypeStruct(SIDE_MSG, jnp.int16)
    flat = row_interval.reshape(1, row_count)
    where = place.astype(jnp.int32).reshape(1)
    plain = [pltpu.VMEM((n, n), F32)]
    work = scratch_of(n)

    space = pl.BlockSpec(memory_space=pltpu.VMEM)
    turned, *parts = pl.pallas_call(
        gram_matrix,
        out_shape=(jax.ShapeDtypeStruct((n, row_count), BF16),) + (matrix_msg,) * SLOTS,
        in_specs=[pl.BlockSpec(memory_space=pltpu.SMEM), space, space],
    )(where, flat, design)
    for i, m in enumerate(ROUNDS):
        parts[i] = to_seat(parts[i], m)
    side_parts = list(gram(functools.partial(gram_side, 3), (side_msg,) * SLOTS, where, flat, turned, observed))
    for i, m in enumerate(ROUNDS):
        side_parts[i] = to_seat(side_parts[i], m)
    mine = carry(jnp.concatenate([prior_ridge, coupling], axis=0), home, seat)
    left_link = carry(coupling, home, lambda t: seat(t + 1) if t + 1 < count else None)
    right_link = jnp.where(time == count - 1, 0.0, mine[1:2])
    vec = jnp.concatenate([mine[0:1], left_link, right_link, jnp.zeros((5, n), F32)], axis=0)
    block, inverse, near = call(first_matrix, (square, square, matrix_msg), work, *parts, vec)
    low, high = along(near, 1), along(near, -1)
    side, near_side = call(first_side, (square, side_msg), plain, inverse, *side_parts)
    low_side, high_side = along(near_side, 1), along(near_side, -1)
    block_one, inverse_one, up, down = call(
        second_matrix, (square, square, matrix_msg, matrix_msg), work, block, low, high, vec
    )
    far_low, far_high = along(up, 2), along(down, -2)
    side_one, up_side, down_side = call(
        second_side, (square, side_msg, side_msg), plain, inverse_one, side, low_side, high_side, vec
    )
    far_low_side, far_high_side = along(up_side, 2), along(down_side, -2)
    inverse_two = call(third_matrix, square, plain * 2 + work, block_one, low, high, far_low, far_high, vec)
    code, rounded = call(
        third_side, (side_msg, half), plain * 3, inverse_two, side_one, low, high, far_low_side, far_high_side, vec
    )
    states = []
    for m in range(SLOTS):
        states.append(to_arc(rounded if m else code, m))
    picked = jnp.where((row_interval == (place ^ 1))[:, None], design, jnp.zeros((), design.dtype))
    partial = observed.astype(F32) - jnp.dot(picked, states[1], preferred_element_type=F32)
    chunk = row_count // 2
    whole = pl.BlockSpec(memory_space=pltpu.VMEM)
    rows = lambda width: pl.BlockSpec((chunk, width), lambda i: (i, 0))
    solution, residual = pl.pallas_call(
        predict,
        grid=(2,),
        out_shape=(square, jax.ShapeDtypeStruct((row_count, n), F32)),
        in_specs=[pl.BlockSpec(memory_space=pltpu.SMEM), rows(1), rows(n), rows(n), whole, whole, whole],
        out_specs=(pl.BlockSpec((n, n), lambda i: (0, 0)), rows(n)),
        scratch_shapes=[pltpu.VMEM((3 * n, n), BF16)],
    )(where, row_interval.reshape(row_count, 1), design, partial, states[0], states[2], states[3])
    return (solution[None], residual)


def solution(mesh):
    placed = (P(PAIR, None), P(PAIR, None), P(PAIR), P(PAIR, None), P(PAIR, None))
    return jax.shard_map(
        step_of,
        mesh=mesh,
        in_specs=placed,
        out_specs=(P(PAIR, None, None), P(PAIR, None)),
        check_vma=False,
    )
```
